256 devices in a mesh: blk: 32 (over z_hi, y, core), head: 8 (over z_lo, x).
Axes of the slice: x: 4, y: 4, z: 8 (z_hi: 4, z_lo: 2; z = z_hi * 2 + z_lo), core: 2. Of those that a mesh axis runs over, the one named last changes fastest.
Arguments:
- query: bfloat16 [32768, 3072], P(('blk', 'head')), may hold values from -6 to 6
- keys: bfloat16 [32768, 3072], P(('blk', 'head')), may hold values from -6 to 6
- values: bfloat16 [32768, 3072], P(('blk', 'head')), may hold values from -6 to 6
- cotangent: bfloat16 [32768, 3072], P(('blk', 'head')), may hold values from -6 to 6
- kv_tiles: int32 [24, 256, 9], P('head'), may hold values from 0 to 255, as said below
Outputs:
- attended: bfloat16 [32768, 3072], P(('blk', 'head'))
- d_query: bfloat16 [32768, 3072], P(('blk', 'head'))
- d_keys: bfloat16 [32768, 3072], P(('blk', 'head'))
- d_values: bfloat16 [32768, 3072], P(('blk', 'head'))
The draws below stay inside these ranges and needn't reach their ends.
Inputs may be any that keep to these rules, and one draw needn't show every extreme that they name: `kv_tiles`: the 9 entries of a row are distinct; the first 2 entries are the same in every row of one head (that head's global tiles); every other entry lies within 8 tiles of the row's query tile and is not a global tile of that head.
All inputs are finite; a program needn't handle non-finite values.
Results may differ from the reference program's by a relative error of at most 0.017.
Values may be sent and summed in bfloat16 or wider, within the bound.
A program may use at most 192 MiB of HBM per device.

```python
import jax
import jax.numpy as jnp
from jax import lax

HEADS = 24
HD = 128
D = 3072
TILE = 128
KSEL = 9
GLOBALS = 2
HALF = 8
SEQ = 32768
QTILES = 256


def draw_query(key, part):
    inner = jax.random.fold_in(key, 1)
    base = jnp.clip(jax.random.normal(inner, (SEQ, D), jnp.float32), -6.0, 6.0)
    return base.astype(jnp.bfloat16)


def draw_keys(key, part):
    inner = jax.random.fold_in(key, 2)
    base = jnp.clip(jax.random.normal(inner, (SEQ, D), jnp.float32), -6.0, 6.0)
    return base.astype(jnp.bfloat16)


def tile_choice(key):
    tiles = jnp.arange(QTILES, dtype=jnp.int32)
    global_score = jax.random.randint(jax.random.fold_in(key, 11), (HEADS, QTILES), 0, 65536) * QTILES + tiles[None, :]
    chosen_globals = lax.top_k(global_score, GLOBALS)[1].astype(jnp.int32)
    width = 2 * HALF + 1
    offsets = jnp.arange(width, dtype=jnp.int32)
    candidate = tiles[:, None] - HALF + offsets[None, :]
    inside = (candidate >= 0) & (candidate < QTILES)
    is_global = jnp.any(candidate[None, :, :, None] == chosen_globals[:, None, None, :], axis=-1)
    usable = inside[None, :, :] & jnp.logical_not(is_global)
    noise = jax.random.randint(jax.random.fold_in(key, 12), (HEADS, QTILES, width), 0, 65536)
    score = jnp.where(usable, noise * width + offsets[None, None, :], -(offsets[None, None, :] + 1))
    picked = lax.top_k(score, KSEL - GLOBALS)[1]
    local_tiles = jnp.take_along_axis(jnp.broadcast_to(candidate[None], (HEADS, QTILES, width)), picked, axis=-1)
    head_globals = jnp.broadcast_to(chosen_globals[:, None, :], (HEADS, QTILES, GLOBALS))
    rows = jnp.concatenate([head_globals, local_tiles.astype(jnp.int32)], axis=-1)
    return rows.astype(jnp.int32)


def draw_kv_tiles(key, part):
    return tile_choice(key)


def block_levels(key, dims, shards, low, largest):
    def one(axis_at, shards_of):
        draws = jax.random.uniform(jax.random.fold_in(jax.random.fold_in(key, 6), axis_at), (shards_of,), jnp.float32, low / len(shards), largest / len(shards))
        return jnp.repeat(jnp.exp(draws), dims[axis_at] // shards_of).reshape((-1,) + (1,) * (len(dims) - axis_at - 1))

    gain = one(*shards[0])
    for cut in shards[1:]:
        gain = gain * one(*cut)
    return gain


def scatter_about(key, dims, deviation, reach, cuts=(), kind=jnp.bfloat16):
    level = block_levels(key, dims, cuts, -0.22, 0.18) if cuts else 1.0
    result = jax.random.normal(key, dims, jnp.float32) * deviation * level
    return jnp.minimum(jnp.maximum(result, -reach), reach).astype(kind)


def setup_inputs(seed: int = 0) -> dict:
    splits = jax.random.split(jax.random.key(seed), 6)
    query = draw_query(jax.random.fold_in(splits[5], 71), 0)
    keys = draw_keys(jax.random.fold_in(splits[5], 71), 0)
    values = scatter_about(splits[2], (SEQ, D), 1.0, 6.0, ((0, 256),))
    cotangent = scatter_about(splits[3], (SEQ, D), 1.0, 6.0, ((0, 256),))
    kv_tiles = draw_kv_tiles(jax.random.fold_in(splits[5], 71), 0)
    return dict(query=query, keys=keys, values=values, cotangent=cotangent, kv_tiles=kv_tiles)


def to_heads(field):
    return field.reshape(QTILES, TILE, HEADS, HD).transpose(2, 0, 1, 3)


def from_heads(field):
    return field.transpose(1, 2, 0, 3).reshape(SEQ, HEADS * HD)


def head_pass(item):
    queries, keys_h, values_h, grad_out, index = item
    scale = HD ** -0.5
    highest = lax.Precision.HIGHEST
    query_f = queries.astype(jnp.float32)
    grad_f = grad_out.astype(jnp.float32)
    chosen_keys = keys_h[index].astype(jnp.float32)
    chosen_values = values_h[index].astype(jnp.float32)
    scores = jnp.einsum("tqd,tskd->tqsk", query_f, chosen_keys, precision=highest) * scale
    peak = jnp.max(scores, axis=(2, 3), keepdims=True)
    log_total = peak + jnp.log(jnp.sum(jnp.exp(scores - peak), axis=(2, 3), keepdims=True))
    probs = jnp.exp(scores - log_total)
    weights = probs.astype(jnp.bfloat16).astype(jnp.float32)
    attended = jnp.einsum("tqsk,tskd->tqd", weights, chosen_values, precision=highest).astype(jnp.bfloat16)
    delta = jnp.sum(grad_f * attended.astype(jnp.float32), axis=-1)
    grad_probs = jnp.einsum("tqd,tskd->tqsk", grad_f, chosen_values, precision=highest)
    grad_scores = (probs * (grad_probs - delta[:, :, None, None])).astype(jnp.bfloat16).astype(jnp.float32)
    grad_query = (jnp.einsum("tqsk,tskd->tqd", grad_scores, chosen_keys, precision=highest) * scale).astype(jnp.bfloat16)
    key_slots = jnp.einsum("tqsk,tqd->tskd", grad_scores, query_f, precision=highest) * scale
    value_slots = jnp.einsum("tqsk,tqd->tskd", weights, grad_f, precision=highest)
    flat = index.reshape(-1).astype(jnp.int32)
    key_grad = jnp.zeros((QTILES, TILE, HD), jnp.float32).at[flat].add(key_slots.reshape(-1, TILE, HD))
    value_grad = jnp.zeros((QTILES, TILE, HD), jnp.float32).at[flat].add(value_slots.reshape(-1, TILE, HD))
    return attended, grad_query, key_grad.astype(jnp.bfloat16), value_grad.astype(jnp.bfloat16)


def reference(query, keys, values, cotangent, kv_tiles):
    results = lax.map(head_pass, (to_heads(query), to_heads(keys), to_heads(values), to_heads(cotangent), kv_tiles))
    return (from_heads(results[0]), from_heads(results[1]), from_heads(results[2]), from_heads(results[3]))
```

```python
import jax
import jax.numpy as jnp
from jax import lax
from jax.sharding import PartitionSpec as P

HD = 128
TILE = 128
GLOBALS = 2
HALF = 8


def passed_along(block, axis, distance):
    devices = range(lax.axis_size(axis))
    route = [(i - distance, i) for i in devices if i - distance in devices]
    return lax.ppermute(block, axis, route)


def butterfly_sum(block, axis):
    count = lax.axis_size(axis)
    if count & (count - 1):
        return lax.psum(block, axis)
    stride = 1
    while stride < count:
        route = [(i, i ^ stride) for i in range(count)]
        block = block + lax.ppermute(block, axis, route)
        stride *= 2
    return block


def split_heads(field, count):
    heads = field.shape[1] // HD
    return field.reshape(count, TILE, heads, HD).transpose(2, 0, 1, 3)


def merge_heads(field):
    heads = field.shape[0]
    count = field.shape[1]
    return field.transpose(1, 2, 0, 3).reshape(count * TILE, heads * HD)


def recompute_probs(queries, chosen_keys, log_total):
    scale = HD ** (-0.5)
    scores = (
        jnp.einsum("tqd,tskd->tqsk", queries, chosen_keys, preferred_element_type=jnp.float32)
        * scale
    )
    return jnp.exp(scores - log_total)


def attend_forward(item):
    queries, pool_keys, pool_values, pool_index = item
    scale = HD ** (-0.5)
    chosen_keys = jnp.take(pool_keys, pool_index, axis=0)
    chosen_values = jnp.take(pool_values, pool_index, axis=0)
    scores = (
        jnp.einsum("tqd,tskd->tqsk", queries, chosen_keys, preferred_element_type=jnp.float32)
        * scale
    )
    peak = jnp.max(scores, axis=(2, 3), keepdims=True)
    log_total = peak + jnp.log(jnp.sum(jnp.exp(scores - peak), axis=(2, 3), keepdims=True))
    weights = jnp.exp(scores - log_total).astype(jnp.bfloat16)
    attended = jnp.einsum(
        "tqsk,tskd->tqd", weights, chosen_values, preferred_element_type=jnp.float32
    )
    return (attended.astype(jnp.bfloat16), log_total)


def attend_backward(item):
    queries, pool_keys, pool_values, grad_out, attended, log_total, pool_index = item
    scale = HD ** (-0.5)
    chosen_keys = jnp.take(pool_keys, pool_index, axis=0)
    chosen_values = jnp.take(pool_values, pool_index, axis=0)
    probs = recompute_probs(queries, chosen_keys, log_total)
    weights = probs.astype(jnp.bfloat16)
    delta = jnp.sum(grad_out.astype(jnp.float32) * attended.astype(jnp.float32), axis=-1)
    grad_probs = jnp.einsum(
        "tqd,tskd->tqsk", grad_out, chosen_values, preferred_element_type=jnp.float32
    )
    grad_scores = (probs * (grad_probs - delta[:, :, None, None])).astype(jnp.bfloat16)
    grad_query = (
        jnp.einsum("tqsk,tskd->tqd", grad_scores, chosen_keys, preferred_element_type=jnp.float32)
        * scale
    )
    key_slots = (
        jnp.einsum("tqsk,tqd->tskd", grad_scores, queries, preferred_element_type=jnp.float32)
        * scale
    )
    value_slots = jnp.einsum(
        "tqsk,tqd->tskd", weights, grad_out, preferred_element_type=jnp.float32
    )
    slot_count = pool_index.shape[0] * pool_index.shape[1]
    places = (
        pool_index.reshape(-1)[:, None] == jnp.arange(pool_keys.shape[0], dtype=jnp.int32)[None, :]
    ).astype(jnp.float32)
    key_pool = jnp.einsum(
        "sp,skd->pkd",
        places,
        key_slots.reshape(slot_count, TILE, HD),
        precision=lax.Precision.HIGHEST,
    )
    value_pool = jnp.einsum(
        "sp,skd->pkd",
        places,
        value_slots.reshape(slot_count, TILE, HD),
        precision=lax.Precision.HIGHEST,
    )
    return (grad_query.astype(jnp.bfloat16), key_pool, value_pool)


def per_device(query, keys, values, cotangent, kv_tiles):
    head_count = lax.axis_size("head")
    cycle_pos = lax.axis_index("blk")
    per_frame = query.shape[0] * head_count // TILE
    reach = -(-HALF // per_frame)
    span = (2 * reach + 1) * per_frame
    global_tiles = kv_tiles[:, 0, :GLOBALS]
    own_tiles = lax.dynamic_slice_in_dim(kv_tiles, cycle_pos * per_frame, per_frame, 1)
    moved = (
        lax.all_to_all(query, "head", split_axis=1, concat_axis=0, tiled=True),
        lax.all_to_all(keys, "head", split_axis=1, concat_axis=0, tiled=True),
        lax.all_to_all(values, "head", split_axis=1, concat_axis=0, tiled=True),
        lax.all_to_all(cotangent, "head", split_axis=1, concat_axis=0, tiled=True),
    )
    frame_keys = moved[1]
    frame_values = moved[2]
    offset = 1
    earlier = passed_along((frame_keys, frame_values), "blk", offset)
    later = passed_along((frame_keys, frame_values), "blk", -offset)
    earlier_keys = [earlier[0]]
    earlier_values = [earlier[1]]
    later_keys = [later[0]]
    later_values = [later[1]]
    near_keys = jnp.stack(earlier_keys[::-1] + later_keys, axis=0)
    near_values = jnp.stack(earlier_values[::-1] + later_values, axis=0)
    width = frame_keys.shape[1]
    all_keys = jnp.concatenate(
        [near_keys[:reach], frame_keys[None], near_keys[reach:]], axis=0
    ).reshape(span * TILE, width)
    all_values = jnp.concatenate(
        [near_values[:reach], frame_values[None], near_values[reach:]], axis=0
    ).reshape(span * TILE, width)
    own_keys = split_heads(frame_keys, per_frame)
    own_values = split_heads(frame_values, per_frame)
    tile_ids = cycle_pos * per_frame + jnp.arange(per_frame, dtype=jnp.int32)
    owner = global_tiles[:, :, None] == tile_ids[None, None, :]
    owner_mask = owner.astype(jnp.bfloat16)
    global_keys = jnp.einsum(
        "hjt,htkd->hjkd", owner_mask, own_keys, preferred_element_type=jnp.float32
    )
    global_values = jnp.einsum(
        "hjt,htkd->hjkd", owner_mask, own_values, preferred_element_type=jnp.float32
    )
    global_both = butterfly_sum(
        jnp.stack([global_keys.astype(jnp.bfloat16), global_values.astype(jnp.bfloat16)]), "blk"
    ).astype(jnp.float32)
    global_keys, global_values = global_both[0], global_both[1]
    pool_keys = jnp.concatenate(
        [split_heads(all_keys, span), global_keys.astype(jnp.bfloat16)], axis=1
    )
    pool_values = jnp.concatenate(
        [split_heads(all_values, span), global_values.astype(jnp.bfloat16)], axis=1
    )
    relative = own_tiles - (cycle_pos - reach) * per_frame
    inside = (relative >= 0) & (relative < span)
    matches = own_tiles[:, :, :, None] == global_tiles[:, None, None, :]
    slot_numbers = jnp.arange(global_tiles.shape[1], dtype=jnp.int32)
    global_slot = jnp.sum(jnp.where(matches, slot_numbers[None, None, None, :], 0), axis=-1)
    pool_index = jnp.where(inside, relative, span + global_slot)
    queries = split_heads(moved[0], per_frame)
    grad_out = split_heads(moved[3], per_frame)
    attended, log_total = lax.map(attend_forward, (queries, pool_keys, pool_values, pool_index))
    grad_query, key_pool, value_pool = lax.map(
        attend_backward,
        (queries, pool_keys, pool_values, grad_out, attended, log_total, pool_index),
    )
    centre = reach * per_frame
    key_grad = key_pool[:, centre : centre + per_frame]
    value_grad = value_pool[:, centre : centre + per_frame]
    offset = 1
    lower = (reach - offset) * per_frame
    returned = (
        passed_along(
            key_pool[:, lower : lower + per_frame].astype(jnp.bfloat16), "blk", -offset
        ).astype(jnp.float32),
        passed_along(
            value_pool[:, lower : lower + per_frame].astype(jnp.bfloat16), "blk", -offset
        ).astype(jnp.float32),
    )
    key_grad = key_grad + returned[0]
    value_grad = value_grad + returned[1]
    upper = (reach + offset) * per_frame
    returned = (
        passed_along(
            key_pool[:, upper : upper + per_frame].astype(jnp.bfloat16), "blk", offset
        ).astype(jnp.float32),
        passed_along(
            value_pool[:, upper : upper + per_frame].astype(jnp.bfloat16), "blk", offset
        ).astype(jnp.float32),
    )
    key_grad = key_grad + returned[0]
    value_grad = value_grad + returned[1]
    summed = butterfly_sum(jnp.stack([key_pool[:, span:], value_pool[:, span:]]), "blk")
    owner_float = owner.astype(jnp.float32)
    key_grad = key_grad + jnp.einsum(
        "hjt,hjkd->htkd", owner_float, summed[0], precision=lax.Precision.HIGHEST
    )
    value_grad = value_grad + jnp.einsum(
        "hjt,hjkd->htkd", owner_float, summed[1], precision=lax.Precision.HIGHEST
    )
    query_rows = merge_heads(grad_query)
    key_rows = merge_heads(key_grad.astype(jnp.bfloat16))
    value_rows = merge_heads(value_grad.astype(jnp.bfloat16))
    results = (
        lax.all_to_all(merge_heads(attended), "head", split_axis=0, concat_axis=1, tiled=True),
        lax.all_to_all(query_rows, "head", split_axis=0, concat_axis=1, tiled=True),
        lax.all_to_all(key_rows, "head", split_axis=0, concat_axis=1, tiled=True),
        lax.all_to_all(value_rows, "head", split_axis=0, concat_axis=1, tiled=True),
    )
    return (results[0], results[1], results[2], results[3])


def solution(mesh):
    placed = (
        P(("blk", "head"), None),
        P(("blk", "head"), None),
        P(("blk", "head"), None),
        P(("blk", "head"), None),
        P("head", None, None),
    )
    return jax.shard_map(
        per_device,
        mesh=mesh,
        in_specs=placed,
        out_specs=(
            P(("blk", "head"), None),
            P(("blk", "head"), None),
            P(("blk", "head"), None),
            P(("blk", "head"), None),
        ),
        check_vma=False,
    )
```

```python
import jax
import jax.numpy as jnp
from jax import lax
from jax.experimental import pallas as pl
from jax.experimental.pallas import tpu as pltpu
from jax.sharding import PartitionSpec as P

HD = 128
TILE = 128
GLOBALS = 2
HALF = 8


def passed_along(block, axis, distance):
    devices = range(lax.axis_size(axis))
    route = [(i - distance, i) for i in devices if i - distance in devices]
    return lax.ppermute(block, axis, route)


def butterfly_sum(block, axis):
    count = lax.axis_size(axis)
    if count & (count - 1):
        return lax.psum(block, axis)
    stride = 1
    while stride < count:
        route = [(i, i ^ stride) for i in range(count)]
        block = block + lax.ppermute(block, axis, route)
        stride *= 2
    return block


def split_heads(field, count):
    heads = field.shape[1] // HD
    return field.reshape(count, TILE, heads, HD).transpose(2, 0, 1, 3)


def merge_heads(field):
    heads = field.shape[0]
    count = field.shape[1]
    return field.transpose(1, 2, 0, 3).reshape(count * TILE, heads * HD)


def attention_kernel(index_ref, q_ref, do_ref, k_ref, v_ref, att_ref, dq_ref, dk_ref, dv_ref, kbuf, vbuf):
    heads = q_ref.shape[1] // HD
    tiles = q_ref.shape[0] // TILE
    slots = index_ref.shape[0] // (heads * tiles)
    scale = HD ** (-0.5)
    dk_ref[...] = jnp.zeros_like(dk_ref)
    dv_ref[...] = jnp.zeros_like(dv_ref)
    nt = (((1,), (1,)), ((), ()))
    tn = (((0,), (0,)), ((), ()))

    def step(item, carry):
        head = item // tiles
        tile = item % tiles
        cols = pl.ds(pl.multiple_of(head * HD, HD), HD)
        rows = pl.ds(pl.multiple_of(tile * TILE, TILE), TILE)
        picks = [
            pl.ds(pl.multiple_of(index_ref[item * slots + s] * TILE, TILE), TILE)
            for s in range(slots)
        ]
        for s in range(slots):
            kbuf[s * TILE : (s + 1) * TILE, :] = k_ref[picks[s], cols]
            vbuf[s * TILE : (s + 1) * TILE, :] = v_ref[picks[s], cols]
        query = q_ref[rows, cols]
        grad_out = do_ref[rows, cols]
        chosen_keys = kbuf[...]
        chosen_values = vbuf[...]
        scores = (
            lax.dot_general(query, chosen_keys, nt, preferred_element_type=jnp.float32) * scale
        )
        peak = jnp.max(scores, axis=1, keepdims=True)
        log_total = peak + jnp.log(jnp.sum(jnp.exp(scores - peak), axis=1, keepdims=True))
        probs = jnp.exp(scores - log_total)
        weights = probs.astype(jnp.bfloat16)
        attended = jnp.dot(weights, chosen_values, preferred_element_type=jnp.float32).astype(
            jnp.bfloat16
        )
        att_ref[rows, cols] = attended
        delta = jnp.sum(
            grad_out.astype(jnp.float32) * attended.astype(jnp.float32), axis=1, keepdims=True
        )
        grad_probs = lax.dot_general(
            grad_out, chosen_values, nt, preferred_element_type=jnp.float32
        )
        grad_scores = (probs * (grad_probs - delta)).astype(jnp.bfloat16)
        dq_ref[rows, cols] = (
            jnp.dot(grad_scores, chosen_keys, preferred_element_type=jnp.float32) * scale
        ).astype(jnp.bfloat16)
        key_slots = (
            lax.dot_general(grad_scores, query, tn, preferred_element_type=jnp.float32) * scale
        )
        value_slots = lax.dot_general(weights, grad_out, tn, preferred_element_type=jnp.float32)
        for s in range(slots):
            dk_ref[picks[s], cols] += key_slots[s * TILE : (s + 1) * TILE]
            dv_ref[picks[s], cols] += value_slots[s * TILE : (s + 1) * TILE]
        return carry

    lax.fori_loop(0, heads * tiles, step, 0)


def attend(pool_index, query_rows, grad_rows, pool_keys, pool_values):
    count, width = query_rows.shape
    pool_rows = pool_keys.shape[0]
    slots = pool_index.shape[-1]
    vmem = pltpu.VMEM
    flops = 2 * 7 * count * slots * TILE * width
    return pl.pallas_call(
        attention_kernel,
        out_shape=(
            jax.ShapeDtypeStruct((count, width), jnp.bfloat16),
            jax.ShapeDtypeStruct((count, width), jnp.bfloat16),
            jax.ShapeDtypeStruct((pool_rows, width), jnp.float32),
            jax.ShapeDtypeStruct((pool_rows, width), jnp.float32),
        ),
        in_specs=[pl.BlockSpec(memory_space=pltpu.SMEM)] + [pl.BlockSpec(memory_space=vmem)] * 4,
        out_specs=tuple(pl.BlockSpec(memory_space=vmem) for _ in range(4)),
        scratch_shapes=[
            pltpu.VMEM((slots * TILE, HD), jnp.bfloat16),
            pltpu.VMEM((slots * TILE, HD), jnp.bfloat16),
        ],
        compiler_params=pltpu.CompilerParams(vmem_limit_bytes=60 * 1024 * 1024),
        cost_estimate=pl.CostEstimate(
            flops=flops,
            transcendentals=count * slots * TILE * width // HD,
            bytes_accessed=8 * count * width + 12 * pool_rows * width,
        ),
    )(pool_index.reshape(-1), query_rows, grad_rows, pool_keys, pool_values)


def per_device(query, keys, values, cotangent, kv_tiles):
    head_count = lax.axis_size("head")
    cycle_pos = lax.axis_index("blk")
    per_frame = query.shape[0] * head_count // TILE
    reach = -(-HALF // per_frame)
    span = (2 * reach + 1) * per_frame
    global_tiles = kv_tiles[:, 0, :GLOBALS]
    own_tiles = lax.dynamic_slice_in_dim(kv_tiles, cycle_pos * per_frame, per_frame, 1)
    moved = (
        lax.all_to_all(query, "head", split_axis=1, concat_axis=0, tiled=True),
        lax.all_to_all(keys, "head", split_axis=1, concat_axis=0, tiled=True),
        lax.all_to_all(values, "head", split_axis=1, concat_axis=0, tiled=True),
        lax.all_to_all(cotangent, "head", split_axis=1, concat_axis=0, tiled=True),
    )
    frame_keys = moved[1]
    frame_values = moved[2]
    offset = 1
    earlier = passed_along((frame_keys, frame_values), "blk", offset)
    later = passed_along((frame_keys, frame_values), "blk", -offset)
    earlier_keys = [earlier[0]]
    earlier_values = [earlier[1]]
    later_keys = [later[0]]
    later_values = [later[1]]
    near_keys = jnp.stack(earlier_keys[::-1] + later_keys, axis=0)
    near_values = jnp.stack(earlier_values[::-1] + later_values, axis=0)
    width = frame_keys.shape[1]
    all_keys = jnp.concatenate(
        [near_keys[:reach], frame_keys[None], near_keys[reach:]], axis=0
    ).reshape(span * TILE, width)
    all_values = jnp.concatenate(
        [near_values[:reach], frame_values[None], near_values[reach:]], axis=0
    ).reshape(span * TILE, width)
    heads = width // HD
    tile_ids = cycle_pos * per_frame + jnp.arange(per_frame, dtype=jnp.int32)
    owner = global_tiles[:, :, None] == tile_ids[None, None, :]
    owner_mask = owner.astype(jnp.bfloat16)
    frame_key_tiles = frame_keys.reshape(per_frame, TILE, heads, HD)
    frame_value_tiles = frame_values.reshape(per_frame, TILE, heads, HD)
    global_keys = jnp.einsum(
        "hjt,tkhd->jkhd", owner_mask, frame_key_tiles, preferred_element_type=jnp.float32
    )
    global_values = jnp.einsum(
        "hjt,tkhd->jkhd", owner_mask, frame_value_tiles, preferred_element_type=jnp.float32
    )
    global_both = butterfly_sum(
        jnp.stack([global_keys.astype(jnp.bfloat16), global_values.astype(jnp.bfloat16)]), "blk"
    )
    global_rows = GLOBALS * TILE
    pool_keys = jnp.concatenate([all_keys, global_both[0].reshape(global_rows, width)], axis=0)
    pool_values = jnp.concatenate([all_values, global_both[1].reshape(global_rows, width)], axis=0)
    relative = own_tiles - (cycle_pos - reach) * per_frame
    inside = (relative >= 0) & (relative < span)
    matches = own_tiles[:, :, :, None] == global_tiles[:, None, None, :]
    slot_numbers = jnp.arange(global_tiles.shape[1], dtype=jnp.int32)
    global_slot = jnp.sum(jnp.where(matches, slot_numbers[None, None, None, :], 0), axis=-1)
    pool_index = jnp.where(inside, relative, span + global_slot)
    attended, query_rows, key_pool, value_pool = attend(
        pool_index, moved[0], moved[3], pool_keys, pool_values
    )
    frame_rows = per_frame * TILE
    centre = reach * frame_rows
    key_grad = key_pool[centre : centre + frame_rows]
    value_grad = value_pool[centre : centre + frame_rows]
    offset = 1
    lower = (reach - offset) * frame_rows
    returned = (
        passed_along(
            key_pool[lower : lower + frame_rows].astype(jnp.bfloat16), "blk", -offset
        ).astype(jnp.float32),
        passed_along(
            value_pool[lower : lower + frame_rows].astype(jnp.bfloat16), "blk", -offset
        ).astype(jnp.float32),
    )
    key_grad = key_grad + returned[0]
    value_grad = value_grad + returned[1]
    upper = (reach + offset) * frame_rows
    returned = (
        passed_along(
            key_pool[upper : upper + frame_rows].astype(jnp.bfloat16), "blk", offset
        ).astype(jnp.float32),
        passed_along(
            value_pool[upper : upper + frame_rows].astype(jnp.bfloat16), "blk", offset
        ).astype(jnp.float32),
    )
    key_grad = key_grad + returned[0]
    value_grad = value_grad + returned[1]
    pool_end = span * TILE
    summed = butterfly_sum(
        jnp.stack([key_pool[pool_end:], value_pool[pool_end:]]).reshape(
            2, GLOBALS, TILE, heads, HD
        ),
        "blk",
    )
    owner_float = owner.astype(jnp.float32)
    key_grad = key_grad + jnp.einsum(
        "hjt,jkhd->tkhd", owner_float, summed[0], precision=lax.Precision.HIGHEST
    ).reshape(frame_rows, width)
    value_grad = value_grad + jnp.einsum(
        "hjt,jkhd->tkhd", owner_float, summed[1], precision=lax.Precision.HIGHEST
    ).reshape(frame_rows, width)
    key_rows = key_grad.astype(jnp.bfloat16)
    value_rows = value_grad.astype(jnp.bfloat16)
    results = (
        lax.all_to_all(attended, "head", split_axis=0, concat_axis=1, tiled=True),
        lax.all_to_all(query_rows, "head", split_axis=0, concat_axis=1, tiled=True),
        lax.all_to_all(key_rows, "head", split_axis=0, concat_axis=1, tiled=True),
        lax.all_to_all(value_rows, "head", split_axis=0, concat_axis=1, tiled=True),
    )
    return (results[0], results[1], results[2], results[3])


def solution(mesh):
    placed = (
        P(("blk", "head"), None),
        P(("blk", "head"), None),
        P(("blk", "head"), None),
        P(("blk", "head"), None),
        P("head", None, None),
    )
    return jax.shard_map(
        per_device,
        mesh=mesh,
        in_specs=placed,
        out_specs=(
            P(("blk", "head"), None),
            P(("blk", "head"), None),
            P(("blk", "head"), None),
            P(("blk", "head"), None),
        ),
        check_vma=False,
    )
```

```python
import jax
import jax.numpy as jnp
from jax import lax
from jax.experimental import pallas as pl
from jax.experimental.pallas import tpu as pltpu
from jax.sharding import PartitionSpec as P

HD = 128
TILE = 128
GLOBALS = 2
HALF = 8


def passed_along(block, axis, distance):
    devices = range(lax.axis_size(axis))
    route = [(i - distance, i) for i in devices if i - distance in devices]
    return lax.ppermute(block, axis, route)


def butterfly_sum(block, axis):
    count = lax.axis_size(axis)
    if count & (count - 1) or block.size % count:
        return lax.psum(block, axis)
    me = lax.axis_index(axis)
    shape = block.shape
    piece = block.reshape(-1)
    stride = 1
    while stride < count:
        half = piece.shape[0] // 2
        upper = (me & stride) != 0
        low, high = piece[:half], piece[half:]
        route = [(i, i ^ stride) for i in range(count)]
        sent = lax.ppermute(jnp.where(upper, low, high), axis, route)
        piece = jnp.where(upper, high, low) + sent
        stride *= 2
    while stride > 1:
        stride //= 2
        upper = (me & stride) != 0
        route = [(i, i ^ stride) for i in range(count)]
        got = lax.ppermute(piece, axis, route)
        piece = jnp.where(upper, jnp.concatenate([got, piece]), jnp.concatenate([piece, got]))
    return piece.reshape(shape)


def split_heads(field, count):
    heads = field.shape[1] // HD
    return field.reshape(count, TILE, heads, HD).transpose(2, 0, 1, 3)


def merge_heads(field):
    heads = field.shape[0]
    count = field.shape[1]
    return field.transpose(1, 2, 0, 3).reshape(count * TILE, heads * HD)


def attention_kernel(index_ref, q_ref, do_ref, k_ref, v_ref, att_ref, dq_ref, dk_ref, dv_ref, kbuf, vbuf):
    heads = q_ref.shape[1] // HD
    tiles = q_ref.shape[0] // TILE
    slots = index_ref.shape[0] // (heads * tiles)
    scale = HD ** (-0.5)
    dk_ref[...] = jnp.zeros_like(dk_ref)
    dv_ref[...] = jnp.zeros_like(dv_ref)
    nt = (((1,), (1,)), ((), ()))
    tn = (((0,), (0,)), ((), ()))

    def step(item, carry):
        head = item // tiles
        tile = item % tiles
        cols = pl.ds(pl.multiple_of(head * HD, HD), HD)
        rows = pl.ds(pl.multiple_of(tile * TILE, TILE), TILE)
        picks = [
            pl.ds(pl.multiple_of(index_ref[item * slots + s] * TILE, TILE), TILE)
            for s in range(slots)
        ]
        for s in range(slots):
            kbuf[s * TILE : (s + 1) * TILE, :] = k_ref[picks[s], cols]
            vbuf[s * TILE : (s + 1) * TILE, :] = v_ref[picks[s], cols]
        query = q_ref[rows, cols]
        grad_out = do_ref[rows, cols]
        chosen_keys = kbuf[...]
        chosen_values = vbuf[...]
        scores = (
            lax.dot_general(query, chosen_keys, nt, preferred_element_type=jnp.float32) * scale
        )
        peak = jnp.max(scores, axis=1, keepdims=True)
        log_total = peak + jnp.log(jnp.sum(jnp.exp(scores - peak), axis=1, keepdims=True))
        probs = jnp.exp(scores - log_total)
        weights = probs.astype(jnp.bfloat16)
        attended = jnp.dot(weights, chosen_values, preferred_element_type=jnp.float32).astype(
            jnp.bfloat16
        )
        att_ref[rows, cols] = attended
        delta = jnp.sum(
            grad_out.astype(jnp.float32) * attended.astype(jnp.float32), axis=1, keepdims=True
        )
        grad_probs = lax.dot_general(
            grad_out, chosen_values, nt, preferred_element_type=jnp.float32
        )
        grad_scores = (probs * (grad_probs - delta)).astype(jnp.bfloat16)
        dq_ref[rows, cols] = (
            jnp.dot(grad_scores, chosen_keys, preferred_element_type=jnp.float32) * scale
        ).astype(jnp.bfloat16)
        key_slots = (
            lax.dot_general(grad_scores, query, tn, preferred_element_type=jnp.float32) * scale
        )
        value_slots = lax.dot_general(weights, grad_out, tn, preferred_element_type=jnp.float32)
        for s in range(slots):
            dk_ref[picks[s], cols] += key_slots[s * TILE : (s + 1) * TILE]
            dv_ref[picks[s], cols] += value_slots[s * TILE : (s + 1) * TILE]
        return carry

    lax.fori_loop(0, heads * tiles, step, 0)


def attend(pool_index, query_rows, grad_rows, pool_keys, pool_values):
    count, width = query_rows.shape
    pool_rows = pool_keys.shape[0]
    slots = pool_index.shape[-1]
    vmem = pltpu.VMEM
    flops = 2 * 7 * count * slots * TILE * width
    return pl.pallas_call(
        attention_kernel,
        out_shape=(
            jax.ShapeDtypeStruct((count, width), jnp.bfloat16),
            jax.ShapeDtypeStruct((count, width), jnp.bfloat16),
            jax.ShapeDtypeStruct((pool_rows, width), jnp.float32),
            jax.ShapeDtypeStruct((pool_rows, width), jnp.float32),
        ),
        in_specs=[pl.BlockSpec(memory_space=pltpu.SMEM)] + [pl.BlockSpec(memory_space=vmem)] * 4,
        out_specs=tuple(pl.BlockSpec(memory_space=vmem) for _ in range(4)),
        scratch_shapes=[
            pltpu.VMEM((slots * TILE, HD), jnp.bfloat16),
            pltpu.VMEM((slots * TILE, HD), jnp.bfloat16),
        ],
        compiler_params=pltpu.CompilerParams(vmem_limit_bytes=60 * 1024 * 1024),
        cost_estimate=pl.CostEstimate(
            flops=flops,
            transcendentals=count * slots * TILE * width // HD,
            bytes_accessed=8 * count * width + 12 * pool_rows * width,
        ),
    )(pool_index.reshape(-1), query_rows, grad_rows, pool_keys, pool_values)


def per_device(query, keys, values, cotangent, kv_tiles):
    head_count = lax.axis_size("head")
    cycle_pos = lax.axis_index("blk")
    per_frame = query.shape[0] * head_count // TILE
    reach = -(-HALF // per_frame)
    span = (2 * reach + 1) * per_frame
    global_tiles = kv_tiles[:, 0, :GLOBALS]
    own_tiles = lax.dynamic_slice_in_dim(kv_tiles, cycle_pos * per_frame, per_frame, 1)
    moved = lax.all_to_all(
        jnp.stack([query, keys, values, cotangent]), "head", split_axis=2, concat_axis=1, tiled=True
    )
    frame_keys = moved[1]
    frame_values = moved[2]
    offset = 1
    earlier = passed_along((frame_keys, frame_values), "blk", offset)
    later = passed_along((frame_keys, frame_values), "blk", -offset)
    earlier_keys = [earlier[0]]
    earlier_values = [earlier[1]]
    later_keys = [later[0]]
    later_values = [later[1]]
    near_keys = jnp.stack(earlier_keys[::-1] + later_keys, axis=0)
    near_values = jnp.stack(earlier_values[::-1] + later_values, axis=0)
    width = frame_keys.shape[1]
    all_keys = jnp.concatenate(
        [near_keys[:reach], frame_keys[None], near_keys[reach:]], axis=0
    ).reshape(span * TILE, width)
    all_values = jnp.concatenate(
        [near_values[:reach], frame_values[None], near_values[reach:]], axis=0
    ).reshape(span * TILE, width)
    heads = width // HD
    tile_ids = cycle_pos * per_frame + jnp.arange(per_frame, dtype=jnp.int32)
    owner = global_tiles[:, :, None] == tile_ids[None, None, :]
    owner_mask = owner.astype(jnp.bfloat16)
    frame_key_tiles = frame_keys.reshape(per_frame, TILE, heads, HD)
    frame_value_tiles = frame_values.reshape(per_frame, TILE, heads, HD)
    global_keys = jnp.einsum(
        "hjt,tkhd->jkhd", owner_mask, frame_key_tiles, preferred_element_type=jnp.float32
    )
    global_values = jnp.einsum(
        "hjt,tkhd->jkhd", owner_mask, frame_value_tiles, preferred_element_type=jnp.float32
    )
    global_both = butterfly_sum(
        jnp.stack([global_keys.astype(jnp.bfloat16), global_values.astype(jnp.bfloat16)]), "blk"
    )
    global_rows = GLOBALS * TILE
    pool_keys = jnp.concatenate([all_keys, global_both[0].reshape(global_rows, width)], axis=0)
    pool_values = jnp.concatenate([all_values, global_both[1].reshape(global_rows, width)], axis=0)
    relative = own_tiles - (cycle_pos - reach) * per_frame
    inside = (relative >= 0) & (relative < span)
    matches = own_tiles[:, :, :, None] == global_tiles[:, None, None, :]
    slot_numbers = jnp.arange(global_tiles.shape[1], dtype=jnp.int32)
    global_slot = jnp.sum(jnp.where(matches, slot_numbers[None, None, None, :], 0), axis=-1)
    pool_index = jnp.where(inside, relative, span + global_slot)
    attended, query_rows, key_pool, value_pool = attend(
        pool_index, moved[0], moved[3], pool_keys, pool_values
    )
    frame_rows = per_frame * TILE
    centre = reach * frame_rows
    key_grad = key_pool[centre : centre + frame_rows]
    value_grad = value_pool[centre : centre + frame_rows]
    offset = 1
    lower = (reach - offset) * frame_rows
    returned = (
        passed_along(
            key_pool[lower : lower + frame_rows].astype(jnp.bfloat16), "blk", -offset
        ).astype(jnp.float32),
        passed_along(
            value_pool[lower : lower + frame_rows].astype(jnp.bfloat16), "blk", -offset
        ).astype(jnp.float32),
    )
    key_grad = key_grad + returned[0]
    value_grad = value_grad + returned[1]
    upper = (reach + offset) * frame_rows
    returned = (
        passed_along(
            key_pool[upper : upper + frame_rows].astype(jnp.bfloat16), "blk", offset
        ).astype(jnp.float32),
        passed_along(
            value_pool[upper : upper + frame_rows].astype(jnp.bfloat16), "blk", offset
        ).astype(jnp.float32),
    )
    key_grad = key_grad + returned[0]
    value_grad = value_grad + returned[1]
    pool_end = span * TILE
    summed = butterfly_sum(
        jnp.stack([key_pool[pool_end:], value_pool[pool_end:]]).reshape(
            2, GLOBALS, TILE, heads, HD
        ),
        "blk",
    )
    owner_float = owner.astype(jnp.float32)
    key_grad = key_grad + jnp.einsum(
        "hjt,jkhd->tkhd", owner_float, summed[0], precision=lax.Precision.HIGHEST
    ).reshape(frame_rows, width)
    value_grad = value_grad + jnp.einsum(
        "hjt,jkhd->tkhd", owner_float, summed[1], precision=lax.Precision.HIGHEST
    ).reshape(frame_rows, width)
    key_rows = key_grad.astype(jnp.bfloat16)
    value_rows = value_grad.astype(jnp.bfloat16)
    forward_back = lax.all_to_all(
        jnp.stack([attended, query_rows]), "head", split_axis=1, concat_axis=2, tiled=True
    )
    backward_back = lax.all_to_all(
        jnp.stack([key_rows, value_rows]), "head", split_axis=1, concat_axis=2, tiled=True
    )
    results = (forward_back[0], forward_back[1], backward_back[0], backward_back[1])
    return (results[0], results[1], results[2], results[3])


def solution(mesh):
    placed = (
        P(("blk", "head"), None),
        P(("blk", "head"), None),
        P(("blk", "head"), None),
        P(("blk", "head"), None),
        P("head", None, None),
    )
    return jax.shard_map(
        per_device,
        mesh=mesh,
        in_specs=placed,
        out_specs=(
            P(("blk", "head"), None),
            P(("blk", "head"), None),
            P(("blk", "head"), None),
            P(("blk", "head"), None),
        ),
        check_vma=False,
    )
```

```python
import jax
import jax.numpy as jnp
from jax import lax
from jax.experimental import pallas as pl
from jax.experimental.pallas import tpu as pltpu
from jax.sharding import PartitionSpec as P

HD = 128
TILE = 128
GLOBALS = 2
HALF = 8


def passed_along(block, axis, distance):
    devices = range(lax.axis_size(axis))
    route = [(i - distance, i) for i in devices if i - distance in devices]
    return lax.ppermute(block, axis, route)


def butterfly_sum(block, axis):
    count = lax.axis_size(axis)
    if block.size % count:
        return lax.psum(block, axis)
    pieces = block.reshape(count, -1)
    parts = lax.all_to_all(pieces, axis, split_axis=0, concat_axis=0, tiled=True)
    mine = jnp.sum(parts.astype(jnp.float32), axis=0).astype(block.dtype)
    spread = jnp.broadcast_to(mine[None], pieces.shape)
    return lax.all_to_all(spread, axis, split_axis=0, concat_axis=0, tiled=True).reshape(block.shape)


def split_heads(field, count):
    heads = field.shape[1] // HD
    return field.reshape(count, TILE, heads, HD).transpose(2, 0, 1, 3)


def merge_heads(field):
    heads = field.shape[0]
    count = field.shape[1]
    return field.transpose(1, 2, 0, 3).reshape(count * TILE, heads * HD)


def attention_kernel(index_ref, q_ref, do_ref, k_ref, v_ref, att_ref, dq_ref, dk_ref, dv_ref, kbuf, vbuf):
    heads = q_ref.shape[1] // HD
    tiles = q_ref.shape[0] // TILE
    slots = index_ref.shape[0] // (heads * tiles)
    scale = HD ** (-0.5)
    dk_ref[...] = jnp.zeros_like(dk_ref)
    dv_ref[...] = jnp.zeros_like(dv_ref)
    nt = (((1,), (1,)), ((), ()))
    tn = (((0,), (0,)), ((), ()))

    def step(item, carry):
        head = item // tiles
        tile = item % tiles
        cols = pl.ds(pl.multiple_of(head * HD, HD), HD)
        rows = pl.ds(pl.multiple_of(tile * TILE, TILE), TILE)
        picks = [
            pl.ds(pl.multiple_of(index_ref[item * slots + s] * TILE, TILE), TILE)
            for s in range(slots)
        ]
        for s in range(slots):
            kbuf[s * TILE : (s + 1) * TILE, :] = k_ref[picks[s], cols]
            vbuf[s * TILE : (s + 1) * TILE, :] = v_ref[picks[s], cols]
        query = q_ref[rows, cols]
        grad_out = do_ref[rows, cols]
        chosen_keys = kbuf[...]
        chosen_values = vbuf[...]
        scores = (
            lax.dot_general(query, chosen_keys, nt, preferred_element_type=jnp.float32) * scale
        )
        peak = jnp.max(scores, axis=1, keepdims=True)
        log_total = peak + jnp.log(jnp.sum(jnp.exp(scores - peak), axis=1, keepdims=True))
        probs = jnp.exp(scores - log_total)
        weights = probs.astype(jnp.bfloat16)
        attended = jnp.dot(weights, chosen_values, preferred_element_type=jnp.float32).astype(
            jnp.bfloat16
        )
        att_ref[rows, cols] = attended
        delta = jnp.sum(
            grad_out.astype(jnp.float32) * attended.astype(jnp.float32), axis=1, keepdims=True
        )
        grad_probs = lax.dot_general(
            grad_out, chosen_values, nt, preferred_element_type=jnp.float32
        )
        grad_scores = (probs * (grad_probs - delta)).astype(jnp.bfloat16)
        dq_ref[rows, cols] = (
            jnp.dot(grad_scores, chosen_keys, preferred_element_type=jnp.float32) * scale
        ).astype(jnp.bfloat16)
        key_slots = (
            lax.dot_general(grad_scores, query, tn, preferred_element_type=jnp.float32) * scale
        )
        value_slots = lax.dot_general(weights, grad_out, tn, preferred_element_type=jnp.float32)
        for s in range(slots):
            dk_ref[picks[s], cols] += key_slots[s * TILE : (s + 1) * TILE]
            dv_ref[picks[s], cols] += value_slots[s * TILE : (s + 1) * TILE]
        return carry

    lax.fori_loop(0, heads * tiles, step, 0)


def attend(pool_index, query_rows, grad_rows, pool_keys, pool_values):
    count, width = query_rows.shape
    pool_rows = pool_keys.shape[0]
    slots = pool_index.shape[-1]
    vmem = pltpu.VMEM
    flops = 2 * 7 * count * slots * TILE * width
    return pl.pallas_call(
        attention_kernel,
        out_shape=(
            jax.ShapeDtypeStruct((count, width), jnp.bfloat16),
            jax.ShapeDtypeStruct((count, width), jnp.bfloat16),
            jax.ShapeDtypeStruct((pool_rows, width), jnp.float32),
            jax.ShapeDtypeStruct((pool_rows, width), jnp.float32),
        ),
        in_specs=[pl.BlockSpec(memory_space=pltpu.SMEM)] + [pl.BlockSpec(memory_space=vmem)] * 4,
        out_specs=tuple(pl.BlockSpec(memory_space=vmem) for _ in range(4)),
        scratch_shapes=[
            pltpu.VMEM((slots * TILE, HD), jnp.bfloat16),
            pltpu.VMEM((slots * TILE, HD), jnp.bfloat16),
        ],
        compiler_params=pltpu.CompilerParams(vmem_limit_bytes=60 * 1024 * 1024),
        cost_estimate=pl.CostEstimate(
            flops=flops,
            transcendentals=count * slots * TILE * width // HD,
            bytes_accessed=8 * count * width + 12 * pool_rows * width,
        ),
    )(pool_index.reshape(-1), query_rows, grad_rows, pool_keys, pool_values)


def per_device(query, keys, values, cotangent, kv_tiles):
    head_count = lax.axis_size("head")
    cycle_pos = lax.axis_index("blk")
    per_frame = query.shape[0] * head_count // TILE
    reach = -(-HALF // per_frame)
    span = (2 * reach + 1) * per_frame
    global_tiles = kv_tiles[:, 0, :GLOBALS]
    own_tiles = lax.dynamic_slice_in_dim(kv_tiles, cycle_pos * per_frame, per_frame, 1)
    moved = lax.all_to_all(
        jnp.stack([query, keys, values, cotangent]), "head", split_axis=2, concat_axis=1, tiled=True
    )
    frame_keys = moved[1]
    frame_values = moved[2]
    offset = 1
    frame_both = jnp.stack([frame_keys, frame_values])
    earlier = passed_along(frame_both, "blk", offset)
    later = passed_along(frame_both, "blk", -offset)
    earlier_keys = [earlier[0]]
    earlier_values = [earlier[1]]
    later_keys = [later[0]]
    later_values = [later[1]]
    near_keys = jnp.stack(earlier_keys[::-1] + later_keys, axis=0)
    near_values = jnp.stack(earlier_values[::-1] + later_values, axis=0)
    width = frame_keys.shape[1]
    all_keys = jnp.concatenate(
        [near_keys[:reach], frame_keys[None], near_keys[reach:]], axis=0
    ).reshape(span * TILE, width)
    all_values = jnp.concatenate(
        [near_values[:reach], frame_values[None], near_values[reach:]], axis=0
    ).reshape(span * TILE, width)
    heads = width // HD
    tile_ids = cycle_pos * per_frame + jnp.arange(per_frame, dtype=jnp.int32)
    owner = global_tiles[:, :, None] == tile_ids[None, None, :]
    owner_mask = owner.astype(jnp.bfloat16)
    frame_key_tiles = frame_keys.reshape(per_frame, TILE, heads, HD)
    frame_value_tiles = frame_values.reshape(per_frame, TILE, heads, HD)
    global_keys = jnp.einsum(
        "hjt,tkhd->jkhd", owner_mask, frame_key_tiles, preferred_element_type=jnp.float32
    )
    global_values = jnp.einsum(
        "hjt,tkhd->jkhd", owner_mask, frame_value_tiles, preferred_element_type=jnp.float32
    )
    global_both = butterfly_sum(
        jnp.stack([global_keys.astype(jnp.bfloat16), global_values.astype(jnp.bfloat16)]), "blk"
    )
    global_rows = GLOBALS * TILE
    pool_keys = jnp.concatenate([all_keys, global_both[0].reshape(global_rows, width)], axis=0)
    pool_values = jnp.concatenate([all_values, global_both[1].reshape(global_rows, width)], axis=0)
    relative = own_tiles - (cycle_pos - reach) * per_frame
    inside = (relative >= 0) & (relative < span)
    matches = own_tiles[:, :, :, None] == global_tiles[:, None, None, :]
    slot_numbers = jnp.arange(global_tiles.shape[1], dtype=jnp.int32)
    global_slot = jnp.sum(jnp.where(matches, slot_numbers[None, None, None, :], 0), axis=-1)
    pool_index = jnp.where(inside, relative, span + global_slot)
    attended, query_rows, key_pool, value_pool = attend(
        pool_index, moved[0], moved[3], pool_keys, pool_values
    )
    frame_rows = per_frame * TILE
    centre = reach * frame_rows
    key_grad = key_pool[centre : centre + frame_rows]
    value_grad = value_pool[centre : centre + frame_rows]
    offset = 1
    lower = (reach - offset) * frame_rows
    returned = passed_along(
        jnp.stack([key_pool[lower : lower + frame_rows], value_pool[lower : lower + frame_rows]]).astype(
            jnp.bfloat16
        ),
        "blk",
        -offset,
    ).astype(jnp.float32)
    key_grad = key_grad + returned[0]
    value_grad = value_grad + returned[1]
    upper = (reach + offset) * frame_rows
    returned = passed_along(
        jnp.stack([key_pool[upper : upper + frame_rows], value_pool[upper : upper + frame_rows]]).astype(
            jnp.bfloat16
        ),
        "blk",
        offset,
    ).astype(jnp.float32)
    key_grad = key_grad + returned[0]
    value_grad = value_grad + returned[1]
    pool_end = span * TILE
    summed = butterfly_sum(
        jnp.stack([key_pool[pool_end:], value_pool[pool_end:]]).reshape(
            2, GLOBALS, TILE, heads, HD
        ),
        "blk",
    )
    owner_float = owner.astype(jnp.float32)
    key_grad = key_grad + jnp.einsum(
        "hjt,jkhd->tkhd", owner_float, summed[0], precision=lax.Precision.HIGHEST
    ).reshape(frame_rows, width)
    value_grad = value_grad + jnp.einsum(
        "hjt,jkhd->tkhd", owner_float, summed[1], precision=lax.Precision.HIGHEST
    ).reshape(frame_rows, width)
    key_rows = key_grad.astype(jnp.bfloat16)
    value_rows = value_grad.astype(jnp.bfloat16)
    forward_back = lax.all_to_all(
        jnp.stack([attended, query_rows]), "head", split_axis=1, concat_axis=2, tiled=True
    )
    backward_back = lax.all_to_all(
        jnp.stack([key_rows, value_rows]), "head", split_axis=1, concat_axis=2, tiled=True
    )
    results = (forward_back[0], forward_back[1], backward_back[0], backward_back[1])
    return (results[0], results[1], results[2], results[3])


def solution(mesh):
    placed = (
        P(("blk", "head"), None),
        P(("blk", "head"), None),
        P(("blk", "head"), None),
        P(("blk", "head"), None),
        P("head", None, None),
    )
    return jax.shard_map(
        per_device,
        mesh=mesh,
        in_specs=placed,
        out_specs=(
            P(("blk", "head"), None),
            P(("blk", "head"), None),
            P(("blk", "head"), None),
            P(("blk", "head"), None),
        ),
        check_vma=False,
    )
```

```python
import functools

import jax
import jax.numpy as jnp
from jax import lax
from jax.experimental import pallas as pl
from jax.experimental.pallas import tpu as pltpu
from jax.sharding import PartitionSpec as P

MESH = pl.DeviceIdType.MESH
HD = 128
TILE = 128
GLOBALS = 2
HALF = 8


def passed_along(block, axis, distance):
    devices = range(lax.axis_size(axis))
    route = [(i - distance, i) for i in devices if i - distance in devices]
    return lax.ppermute(block, axis, route)


def reduce_kernel(count, x_ref, out_ref, inbox, gathered, mine, send_sem, recv_sem, back_send, back_recv):
    me = lax.axis_index("blk")
    column = lax.axis_index("head")
    barrier = pltpu.get_barrier_semaphore()
    for k in range(1, count):
        pl.semaphore_signal(
            barrier, 1, device_id=(lax.rem(me + k, count), column), device_id_type=MESH
        )
    pl.semaphore_wait(barrier, count - 1)
    outgoing = []
    for k in range(1, count):
        peer = lax.rem(me + k, count)
        copy = pltpu.make_async_remote_copy(
            src_ref=x_ref.at[peer],
            dst_ref=inbox.at[me],
            send_sem=send_sem.at[k],
            recv_sem=recv_sem.at[me],
            device_id=(peer, column),
            device_id_type=MESH,
        )
        copy.start()
        outgoing.append(copy)
    total = x_ref[me].astype(jnp.float32)
    for k in range(1, count):
        source = lax.rem(me + count - k, count)
        pltpu.make_async_remote_copy(
            src_ref=x_ref.at[source],
            dst_ref=inbox.at[source],
            send_sem=send_sem.at[k],
            recv_sem=recv_sem.at[source],
            device_id=(source, column),
            device_id_type=MESH,
        ).wait_recv()
        total = total + inbox[source].astype(jnp.float32)
    mine[...] = total.astype(mine.dtype)
    for k in range(1, count):
        peer = lax.rem(me + k, count)
        copy = pltpu.make_async_remote_copy(
            src_ref=mine,
            dst_ref=gathered.at[me],
            send_sem=back_send.at[k],
            recv_sem=back_recv.at[me],
            device_id=(peer, column),
            device_id_type=MESH,
        )
        copy.start()
        outgoing.append(copy)
    gathered[me] = mine[...]
    for k in range(1, count):
        source = lax.rem(me + count - k, count)
        pltpu.make_async_remote_copy(
            src_ref=mine,
            dst_ref=gathered.at[source],
            send_sem=back_send.at[k],
            recv_sem=back_recv.at[source],
            device_id=(source, column),
            device_id_type=MESH,
        ).wait_recv()
    for copy in outgoing:
        copy.wait_send()
    out_ref[...] = gathered[...]


def butterfly_sum(block, axis, collective):
    count = lax.axis_size(axis)
    if block.size % (count * 8 * 128):
        return lax.psum(block, axis)
    pieces = block.reshape(count, -1, 128)
    vmem = pltpu.VMEM
    summed = pl.pallas_call(
        functools.partial(reduce_kernel, count),
        out_shape=jax.ShapeDtypeStruct(pieces.shape, pieces.dtype),
        in_specs=[pl.BlockSpec(memory_space=vmem)],
        out_specs=pl.BlockSpec(memory_space=vmem),
        scratch_shapes=[
            pltpu.VMEM(pieces.shape, pieces.dtype),
            pltpu.VMEM(pieces.shape, pieces.dtype),
            pltpu.VMEM(pieces.shape[1:], pieces.dtype),
            pltpu.SemaphoreType.DMA((count,)),
            pltpu.SemaphoreType.DMA((count,)),
            pltpu.SemaphoreType.DMA((count,)),
            pltpu.SemaphoreType.DMA((count,)),
        ],
        compiler_params=pltpu.CompilerParams(collective_id=collective, has_side_effects=True),
    )(pieces)
    return summed.reshape(block.shape)


def split_heads(field, count):
    heads = field.shape[1] // HD
    return field.reshape(count, TILE, heads, HD).transpose(2, 0, 1, 3)


def merge_heads(field):
    heads = field.shape[0]
    count = field.shape[1]
    return field.transpose(1, 2, 0, 3).reshape(count * TILE, heads * HD)


def attention_kernel(index_ref, q_ref, do_ref, k_ref, v_ref, att_ref, dq_ref, dk_ref, dv_ref, kbuf, vbuf):
    heads = q_ref.shape[1] // HD
    tiles = q_ref.shape[0] // TILE
    slots = index_ref.shape[0] // (heads * tiles)
    scale = HD ** (-0.5)
    dk_ref[...] = jnp.zeros_like(dk_ref)
    dv_ref[...] = jnp.zeros_like(dv_ref)
    nt = (((1,), (1,)), ((), ()))
    tn = (((0,), (0,)), ((), ()))

    def step(item, carry):
        head = item // tiles
        tile = item % tiles
        cols = pl.ds(pl.multiple_of(head * HD, HD), HD)
        rows = pl.ds(pl.multiple_of(tile * TILE, TILE), TILE)
        picks = [
            pl.ds(pl.multiple_of(index_ref[item * slots + s] * TILE, TILE), TILE)
            for s in range(slots)
        ]
        for s in range(slots):
            kbuf[s * TILE : (s + 1) * TILE, :] = k_ref[picks[s], cols]
            vbuf[s * TILE : (s + 1) * TILE, :] = v_ref[picks[s], cols]
        query = q_ref[rows, cols]
        grad_out = do_ref[rows, cols]
        chosen_keys = kbuf[...]
        chosen_values = vbuf[...]
        scores = (
            lax.dot_general(query, chosen_keys, nt, preferred_element_type=jnp.float32) * scale
        )
        peak = jnp.max(scores, axis=1, keepdims=True)
        log_total = peak + jnp.log(jnp.sum(jnp.exp(scores - peak), axis=1, keepdims=True))
        probs = jnp.exp(scores - log_total)
        weights = probs.astype(jnp.bfloat16)
        attended = jnp.dot(weights, chosen_values, preferred_element_type=jnp.float32).astype(
            jnp.bfloat16
        )
        att_ref[rows, cols] = attended
        delta = jnp.sum(
            grad_out.astype(jnp.float32) * attended.astype(jnp.float32), axis=1, keepdims=True
        )
        grad_probs = lax.dot_general(
            grad_out, chosen_values, nt, preferred_element_type=jnp.float32
        )
        grad_scores = (probs * (grad_probs - delta)).astype(jnp.bfloat16)
        dq_ref[rows, cols] = (
            jnp.dot(grad_scores, chosen_keys, preferred_element_type=jnp.float32) * scale
        ).astype(jnp.bfloat16)
        key_slots = (
            lax.dot_general(grad_scores, query, tn, preferred_element_type=jnp.float32) * scale
        )
        value_slots = lax.dot_general(weights, grad_out, tn, preferred_element_type=jnp.float32)
        for s in range(slots):
            dk_ref[picks[s], cols] += key_slots[s * TILE : (s + 1) * TILE]
            dv_ref[picks[s], cols] += value_slots[s * TILE : (s + 1) * TILE]
        return carry

    lax.fori_loop(0, heads * tiles, step, 0)


def attend(pool_index, query_rows, grad_rows, pool_keys, pool_values):
    count, width = query_rows.shape
    pool_rows = pool_keys.shape[0]
    slots = pool_index.shape[-1]
    vmem = pltpu.VMEM
    flops = 2 * 7 * count * slots * TILE * width
    return pl.pallas_call(
        attention_kernel,
        out_shape=(
            jax.ShapeDtypeStruct((count, width), jnp.bfloat16),
            jax.ShapeDtypeStruct((count, width), jnp.bfloat16),
            jax.ShapeDtypeStruct((pool_rows, width), jnp.float32),
            jax.ShapeDtypeStruct((pool_rows, width), jnp.float32),
        ),
        in_specs=[pl.BlockSpec(memory_space=pltpu.SMEM)] + [pl.BlockSpec(memory_space=vmem)] * 4,
        out_specs=tuple(pl.BlockSpec(memory_space=vmem) for _ in range(4)),
        scratch_shapes=[
            pltpu.VMEM((slots * TILE, HD), jnp.bfloat16),
            pltpu.VMEM((slots * TILE, HD), jnp.bfloat16),
        ],
        compiler_params=pltpu.CompilerParams(vmem_limit_bytes=60 * 1024 * 1024),
        cost_estimate=pl.CostEstimate(
            flops=flops,
            transcendentals=count * slots * TILE * width // HD,
            bytes_accessed=8 * count * width + 12 * pool_rows * width,
        ),
    )(pool_index.reshape(-1), query_rows, grad_rows, pool_keys, pool_values)


def per_device(query, keys, values, cotangent, kv_tiles):
    head_count = lax.axis_size("head")
    cycle_pos = lax.axis_index("blk")
    per_frame = query.shape[0] * head_count // TILE
    reach = -(-HALF // per_frame)
    span = (2 * reach + 1) * per_frame
    global_tiles = kv_tiles[:, 0, :GLOBALS]
    own_tiles = lax.dynamic_slice_in_dim(kv_tiles, cycle_pos * per_frame, per_frame, 1)
    moved = lax.all_to_all(
        jnp.stack([query, keys, values, cotangent]), "head", split_axis=2, concat_axis=1, tiled=True
    )
    frame_keys = moved[1]
    frame_values = moved[2]
    offset = 1
    earlier = passed_along((frame_keys, frame_values), "blk", offset)
    later = passed_along((frame_keys, frame_values), "blk", -offset)
    earlier_keys = [earlier[0]]
    earlier_values = [earlier[1]]
    later_keys = [later[0]]
    later_values = [later[1]]
    near_keys = jnp.stack(earlier_keys[::-1] + later_keys, axis=0)
    near_values = jnp.stack(earlier_values[::-1] + later_values, axis=0)
    width = frame_keys.shape[1]
    all_keys = jnp.concatenate(
        [near_keys[:reach], frame_keys[None], near_keys[reach:]], axis=0
    ).reshape(span * TILE, width)
    all_values = jnp.concatenate(
        [near_values[:reach], frame_values[None], near_values[reach:]], axis=0
    ).reshape(span * TILE, width)
    heads = width // HD
    tile_ids = cycle_pos * per_frame + jnp.arange(per_frame, dtype=jnp.int32)
    owner = global_tiles[:, :, None] == tile_ids[None, None, :]
    owner_mask = owner.astype(jnp.bfloat16)
    frame_key_tiles = frame_keys.reshape(per_frame, TILE, heads, HD)
    frame_value_tiles = frame_values.reshape(per_frame, TILE, heads, HD)
    global_keys = jnp.einsum(
        "hjt,tkhd->jkhd", owner_mask, frame_key_tiles, preferred_element_type=jnp.float32
    )
    global_values = jnp.einsum(
        "hjt,tkhd->jkhd", owner_mask, frame_value_tiles, preferred_element_type=jnp.float32
    )
    global_both = butterfly_sum(
        jnp.stack([global_keys.astype(jnp.bfloat16), global_values.astype(jnp.bfloat16)]), "blk", 0
    )
    global_rows = GLOBALS * TILE
    pool_keys = jnp.concatenate([all_keys, global_both[0].reshape(global_rows, width)], axis=0)
    pool_values = jnp.concatenate([all_values, global_both[1].reshape(global_rows, width)], axis=0)
    relative = own_tiles - (cycle_pos - reach) * per_frame
    inside = (relative >= 0) & (relative < span)
    matches = own_tiles[:, :, :, None] == global_tiles[:, None, None, :]
    slot_numbers = jnp.arange(global_tiles.shape[1], dtype=jnp.int32)
    global_slot = jnp.sum(jnp.where(matches, slot_numbers[None, None, None, :], 0), axis=-1)
    pool_index = jnp.where(inside, relative, span + global_slot)
    attended, query_rows, key_pool, value_pool = attend(
        pool_index, moved[0], moved[3], pool_keys, pool_values
    )
    frame_rows = per_frame * TILE
    centre = reach * frame_rows
    key_grad = key_pool[centre : centre + frame_rows]
    value_grad = value_pool[centre : centre + frame_rows]
    offset = 1
    lower = (reach - offset) * frame_rows
    returned = (
        passed_along(
            key_pool[lower : lower + frame_rows].astype(jnp.bfloat16), "blk", -offset
        ).astype(jnp.float32),
        passed_along(
            value_pool[lower : lower + frame_rows].astype(jnp.bfloat16), "blk", -offset
        ).astype(jnp.float32),
    )
    key_grad = key_grad + returned[0]
    value_grad = value_grad + returned[1]
    upper = (reach + offset) * frame_rows
    returned = (
        passed_along(
            key_pool[upper : upper + frame_rows].astype(jnp.bfloat16), "blk", offset
        ).astype(jnp.float32),
        passed_along(
            value_pool[upper : upper + frame_rows].astype(jnp.bfloat16), "blk", offset
        ).astype(jnp.float32),
    )
    key_grad = key_grad + returned[0]
    value_grad = value_grad + returned[1]
    pool_end = span * TILE
    summed = butterfly_sum(
        jnp.stack([key_pool[pool_end:], value_pool[pool_end:]]).reshape(
            2, GLOBALS, TILE, heads, HD
        ),
        "blk",
        1,
    )
    owner_float = owner.astype(jnp.float32)
    key_grad = key_grad + jnp.einsum(
        "hjt,jkhd->tkhd", owner_float, summed[0], precision=lax.Precision.HIGHEST
    ).reshape(frame_rows, width)
    value_grad = value_grad + jnp.einsum(
        "hjt,jkhd->tkhd", owner_float, summed[1], precision=lax.Precision.HIGHEST
    ).reshape(frame_rows, width)
    key_rows = key_grad.astype(jnp.bfloat16)
    value_rows = value_grad.astype(jnp.bfloat16)
    forward_back = lax.all_to_all(
        jnp.stack([attended, query_rows]), "head", split_axis=1, concat_axis=2, tiled=True
    )
    backward_back = lax.all_to_all(
        jnp.stack([key_rows, value_rows]), "head", split_axis=1, concat_axis=2, tiled=True
    )
    results = (forward_back[0], forward_back[1], backward_back[0], backward_back[1])
    return (results[0], results[1], results[2], results[3])


def solution(mesh):
    placed = (
        P(("blk", "head"), None),
        P(("blk", "head"), None),
        P(("blk", "head"), None),
        P(("blk", "head"), None),
        P("head", None, None),
    )
    return jax.shard_map(
        per_device,
        mesh=mesh,
        in_specs=placed,
        out_specs=(
            P(("blk", "head"), None),
            P(("blk", "head"), None),
            P(("blk", "head"), None),
            P(("blk", "head"), None),
        ),
        check_vma=False,
    )
```

```python
import functools

import jax
import jax.numpy as jnp
from jax import lax
from jax.experimental import pallas as pl
from jax.experimental.pallas import tpu as pltpu
from jax.sharding import PartitionSpec as P

MESH = pl.DeviceIdType.MESH
HD = 128
TILE = 128
GLOBALS = 2
HALF = 8


def passed_along(block, axis, distance):
    devices = range(lax.axis_size(axis))
    route = [(i - distance, i) for i in devices if i - distance in devices]
    return lax.ppermute(block, axis, route)


def reduce_kernel(count, x_ref, out_ref, inbox, gathered, mine, send_sem, recv_sem, back_send, back_recv):
    me = lax.axis_index("blk")
    column = lax.axis_index("head")
    barrier = pltpu.get_barrier_semaphore()
    for k in range(1, count):
        pl.semaphore_signal(
            barrier, 1, device_id=(lax.rem(me + k, count), column), device_id_type=MESH
        )
    pl.semaphore_wait(barrier, count - 1)
    outgoing = []
    for k in range(1, count):
        peer = lax.rem(me + k, count)
        copy = pltpu.make_async_remote_copy(
            src_ref=x_ref.at[peer],
            dst_ref=inbox.at[me],
            send_sem=send_sem.at[k],
            recv_sem=recv_sem.at[me],
            device_id=(peer, column),
            device_id_type=MESH,
        )
        copy.start()
        outgoing.append(copy)
    total = x_ref[me].astype(jnp.float32)
    for k in range(1, count):
        source = lax.rem(me + count - k, count)
        pltpu.make_async_remote_copy(
            src_ref=x_ref.at[source],
            dst_ref=inbox.at[source],
            send_sem=send_sem.at[k],
            recv_sem=recv_sem.at[source],
            device_id=(source, column),
            device_id_type=MESH,
        ).wait_recv()
        total = total + inbox[source].astype(jnp.float32)
    mine[...] = total.astype(mine.dtype)
    for k in range(1, count):
        peer = lax.rem(me + k, count)
        copy = pltpu.make_async_remote_copy(
            src_ref=mine,
            dst_ref=gathered.at[me],
            send_sem=back_send.at[k],
            recv_sem=back_recv.at[me],
            device_id=(peer, column),
            device_id_type=MESH,
        )
        copy.start()
        outgoing.append(copy)
    gathered[me] = mine[...]
    for k in range(1, count):
        source = lax.rem(me + count - k, count)
        pltpu.make_async_remote_copy(
            src_ref=mine,
            dst_ref=gathered.at[source],
            send_sem=back_send.at[k],
            recv_sem=back_recv.at[source],
            device_id=(source, column),
            device_id_type=MESH,
        ).wait_recv()
    for copy in outgoing:
        copy.wait_send()
    out_ref[...] = gathered[...]


def butterfly_sum(block, axis, collective):
    count = lax.axis_size(axis)
    if block.size % (count * 8 * 128):
        return lax.psum(block, axis)
    pieces = block.reshape(count, -1, 128)
    vmem = pltpu.VMEM
    summed = pl.pallas_call(
        functools.partial(reduce_kernel, count),
        out_shape=jax.ShapeDtypeStruct(pieces.shape, pieces.dtype),
        in_specs=[pl.BlockSpec(memory_space=vmem)],
        out_specs=pl.BlockSpec(memory_space=vmem),
        scratch_shapes=[
            pltpu.VMEM(pieces.shape, pieces.dtype),
            pltpu.VMEM(pieces.shape, pieces.dtype),
            pltpu.VMEM(pieces.shape[1:], pieces.dtype),
            pltpu.SemaphoreType.DMA((count,)),
            pltpu.SemaphoreType.DMA((count,)),
            pltpu.SemaphoreType.DMA((count,)),
            pltpu.SemaphoreType.DMA((count,)),
        ],
        compiler_params=pltpu.CompilerParams(collective_id=collective, has_side_effects=True),
    )(pieces)
    return summed.reshape(block.shape)


def split_heads(field, count):
    heads = field.shape[1] // HD
    return field.reshape(count, TILE, heads, HD).transpose(2, 0, 1, 3)


def merge_heads(field):
    heads = field.shape[0]
    count = field.shape[1]
    return field.transpose(1, 2, 0, 3).reshape(count * TILE, heads * HD)


def attention_kernel(
    index_ref, q_ref, do_ref, k_ref, v_ref, att_ref, dq_ref, dk_ref, dv_ref, kbuf, vbuf, dkt, dvt
):
    heads = q_ref.shape[1] // HD
    tiles = q_ref.shape[0] // TILE
    slots = index_ref.shape[0] // (heads * tiles)
    pool_tiles = k_ref.shape[0] // TILE
    scale = HD ** (-0.5)
    dkt[...] = jnp.zeros_like(dkt)
    dvt[...] = jnp.zeros_like(dvt)
    nt = (((1,), (1,)), ((), ()))
    tn = (((0,), (0,)), ((), ()))

    def step(item, carry):
        head = item // tiles
        tile = item % tiles
        cols = pl.ds(pl.multiple_of(head * HD, HD), HD)
        rows = pl.ds(pl.multiple_of(tile * TILE, TILE), TILE)
        picks = [
            pl.ds(pl.multiple_of(index_ref[item * slots + s] * TILE, TILE), TILE)
            for s in range(slots)
        ]
        for s in range(slots):
            kbuf[s * TILE : (s + 1) * TILE, :] = k_ref[picks[s], cols]
            vbuf[s * TILE : (s + 1) * TILE, :] = v_ref[picks[s], cols]
        query = q_ref[rows, cols]
        grad_out = do_ref[rows, cols]
        chosen_keys = kbuf[...]
        chosen_values = vbuf[...]
        scores = (
            lax.dot_general(query, chosen_keys, nt, preferred_element_type=jnp.float32) * scale
        )
        peak = jnp.max(scores, axis=1, keepdims=True)
        lifted = jnp.exp(scores - peak)
        probs = lifted * (1.0 / jnp.sum(lifted, axis=1, keepdims=True))
        weights = probs.astype(jnp.bfloat16)
        attended = jnp.dot(weights, chosen_values, preferred_element_type=jnp.float32).astype(
            jnp.bfloat16
        )
        att_ref[rows, cols] = attended
        delta = jnp.sum(
            grad_out.astype(jnp.float32) * attended.astype(jnp.float32), axis=1, keepdims=True
        )
        grad_probs = lax.dot_general(
            grad_out, chosen_values, nt, preferred_element_type=jnp.float32
        )
        grad_scores = (probs * (grad_probs - delta)).astype(jnp.bfloat16)
        dq_ref[rows, cols] = (
            jnp.dot(grad_scores, chosen_keys, preferred_element_type=jnp.float32) * scale
        ).astype(jnp.bfloat16)
        key_slots = (
            lax.dot_general(query, grad_scores, tn, preferred_element_type=jnp.float32) * scale
        )
        value_slots = lax.dot_general(grad_out, weights, tn, preferred_element_type=jnp.float32)
        for s in range(slots):
            dkt[cols, picks[s]] += key_slots[:, s * TILE : (s + 1) * TILE]
            dvt[cols, picks[s]] += value_slots[:, s * TILE : (s + 1) * TILE]
        return carry

    lax.fori_loop(0, heads * tiles, step, 0)

    def flip(item, carry):
        head = item // pool_tiles
        tile = item % pool_tiles
        cols = pl.ds(pl.multiple_of(head * HD, HD), HD)
        rows = pl.ds(pl.multiple_of(tile * TILE, TILE), TILE)
        dk_ref[rows, cols] = dkt[cols, rows].T
        dv_ref[rows, cols] = dvt[cols, rows].T
        return carry

    lax.fori_loop(0, heads * pool_tiles, flip, 0)


def attend(pool_index, query_rows, grad_rows, pool_keys, pool_values):
    count, width = query_rows.shape
    pool_rows = pool_keys.shape[0]
    slots = pool_index.shape[-1]
    vmem = pltpu.VMEM
    flops = 2 * 7 * count * slots * TILE * width
    return pl.pallas_call(
        attention_kernel,
        out_shape=(
            jax.ShapeDtypeStruct((count, width), jnp.bfloat16),
            jax.ShapeDtypeStruct((count, width), jnp.bfloat16),
            jax.ShapeDtypeStruct((pool_rows, width), jnp.float32),
            jax.ShapeDtypeStruct((pool_rows, width), jnp.float32),
        ),
        in_specs=[pl.BlockSpec(memory_space=pltpu.SMEM)] + [pl.BlockSpec(memory_space=vmem)] * 4,
        out_specs=tuple(pl.BlockSpec(memory_space=vmem) for _ in range(4)),
        scratch_shapes=[
            pltpu.VMEM((slots * TILE, HD), jnp.bfloat16),
            pltpu.VMEM((slots * TILE, HD), jnp.bfloat16),
            pltpu.VMEM((width, pool_rows), jnp.float32),
            pltpu.VMEM((width, pool_rows), jnp.float32),
        ],
        compiler_params=pltpu.CompilerParams(vmem_limit_bytes=60 * 1024 * 1024),
        cost_estimate=pl.CostEstimate(
            flops=flops,
            transcendentals=count * slots * TILE * width // HD,
            bytes_accessed=8 * count * width + 12 * pool_rows * width,
        ),
    )(pool_index.reshape(-1), query_rows, grad_rows, pool_keys, pool_values)


def per_device(query, keys, values, cotangent, kv_tiles):
    head_count = lax.axis_size("head")
    cycle_pos = lax.axis_index("blk")
    per_frame = query.shape[0] * head_count // TILE
    reach = -(-HALF // per_frame)
    span = (2 * reach + 1) * per_frame
    global_tiles = kv_tiles[:, 0, :GLOBALS]
    own_tiles = lax.dynamic_slice_in_dim(kv_tiles, cycle_pos * per_frame, per_frame, 1)
    moved = lax.all_to_all(
        jnp.stack([query, keys, values, cotangent]), "head", split_axis=2, concat_axis=1, tiled=True
    )
    frame_keys = moved[1]
    frame_values = moved[2]
    offset = 1
    earlier = passed_along((frame_keys, frame_values), "blk", offset)
    later = passed_along((frame_keys, frame_values), "blk", -offset)
    earlier_keys = [earlier[0]]
    earlier_values = [earlier[1]]
    later_keys = [later[0]]
    later_values = [later[1]]
    near_keys = jnp.stack(earlier_keys[::-1] + later_keys, axis=0)
    near_values = jnp.stack(earlier_values[::-1] + later_values, axis=0)
    width = frame_keys.shape[1]
    all_keys = jnp.concatenate(
        [near_keys[:reach], frame_keys[None], near_keys[reach:]], axis=0
    ).reshape(span * TILE, width)
    all_values = jnp.concatenate(
        [near_values[:reach], frame_values[None], near_values[reach:]], axis=0
    ).reshape(span * TILE, width)
    heads = width // HD
    tile_ids = cycle_pos * per_frame + jnp.arange(per_frame, dtype=jnp.int32)
    owner = global_tiles[:, :, None] == tile_ids[None, None, :]
    owner_mask = owner.astype(jnp.bfloat16)
    frame_key_tiles = frame_keys.reshape(per_frame, TILE, heads, HD)
    frame_value_tiles = frame_values.reshape(per_frame, TILE, heads, HD)
    global_keys = jnp.einsum(
        "hjt,tkhd->jkhd", owner_mask, frame_key_tiles, preferred_element_type=jnp.float32
    )
    global_values = jnp.einsum(
        "hjt,tkhd->jkhd", owner_mask, frame_value_tiles, preferred_element_type=jnp.float32
    )
    global_both = butterfly_sum(
        jnp.stack([global_keys.astype(jnp.bfloat16), global_values.astype(jnp.bfloat16)]), "blk", 0
    )
    global_rows = GLOBALS * TILE
    pool_keys = jnp.concatenate([all_keys, global_both[0].reshape(global_rows, width)], axis=0)
    pool_values = jnp.concatenate([all_values, global_both[1].reshape(global_rows, width)], axis=0)
    relative = own_tiles - (cycle_pos - reach) * per_frame
    inside = (relative >= 0) & (relative < span)
    matches = own_tiles[:, :, :, None] == global_tiles[:, None, None, :]
    slot_numbers = jnp.arange(global_tiles.shape[1], dtype=jnp.int32)
    global_slot = jnp.sum(jnp.where(matches, slot_numbers[None, None, None, :], 0), axis=-1)
    pool_index = jnp.where(inside, relative, span + global_slot)
    attended, query_rows, key_pool, value_pool = attend(
        pool_index, moved[0], moved[3], pool_keys, pool_values
    )
    frame_rows = per_frame * TILE
    centre = reach * frame_rows
    key_grad = key_pool[centre : centre + frame_rows]
    value_grad = value_pool[centre : centre + frame_rows]
    offset = 1
    lower = (reach - offset) * frame_rows
    returned = (
        passed_along(
            key_pool[lower : lower + frame_rows].astype(jnp.bfloat16), "blk", -offset
        ).astype(jnp.float32),
        passed_along(
            value_pool[lower : lower + frame_rows].astype(jnp.bfloat16), "blk", -offset
        ).astype(jnp.float32),
    )
    key_grad = key_grad + returned[0]
    value_grad = value_grad + returned[1]
    upper = (reach + offset) * frame_rows
    returned = (
        passed_along(
            key_pool[upper : upper + frame_rows].astype(jnp.bfloat16), "blk", offset
        ).astype(jnp.float32),
        passed_along(
            value_pool[upper : upper + frame_rows].astype(jnp.bfloat16), "blk", offset
        ).astype(jnp.float32),
    )
    key_grad = key_grad + returned[0]
    value_grad = value_grad + returned[1]
    pool_end = span * TILE
    summed = butterfly_sum(
        jnp.stack([key_pool[pool_end:], value_pool[pool_end:]]).reshape(
            2, GLOBALS, TILE, heads, HD
        ),
        "blk",
        1,
    )
    owner_float = owner.astype(jnp.float32)
    key_grad = key_grad + jnp.einsum(
        "hjt,jkhd->tkhd", owner_float, summed[0], precision=lax.Precision.HIGHEST
    ).reshape(frame_rows, width)
    value_grad = value_grad + jnp.einsum(
        "hjt,jkhd->tkhd", owner_float, summed[1], precision=lax.Precision.HIGHEST
    ).reshape(frame_rows, width)
    key_rows = key_grad.astype(jnp.bfloat16)
    value_rows = value_grad.astype(jnp.bfloat16)
    forward_back = lax.all_to_all(
        jnp.stack([attended, query_rows]), "head", split_axis=1, concat_axis=2, tiled=True
    )
    backward_back = lax.all_to_all(
        jnp.stack([key_rows, value_rows]), "head", split_axis=1, concat_axis=2, tiled=True
    )
    results = (forward_back[0], forward_back[1], backward_back[0], backward_back[1])
    return (results[0], results[1], results[2], results[3])


def solution(mesh):
    placed = (
        P(("blk", "head"), None),
        P(("blk", "head"), None),
        P(("blk", "head"), None),
        P(("blk", "head"), None),
        P("head", None, None),
    )
    return jax.shard_map(
        per_device,
        mesh=mesh,
        in_specs=placed,
        out_specs=(
            P(("blk", "head"), None),
            P(("blk", "head"), None),
            P(("blk", "head"), None),
            P(("blk", "head"), None),
        ),
        check_vma=False,
    )
```

```python
import functools

import jax
import jax.numpy as jnp
from jax import lax
from jax.experimental import pallas as pl
from jax.experimental.pallas import tpu as pltpu
from jax.sharding import PartitionSpec as P

MESH = pl.DeviceIdType.MESH
HD = 128
TILE = 128
GLOBALS = 2
HALF = 8


def passed_along(block, axis, distance):
    devices = range(lax.axis_size(axis))
    route = [(i - distance, i) for i in devices if i - distance in devices]
    return lax.ppermute(block, axis, route)


def reduce_kernel(count, x_ref, out_ref, inbox, gathered, mine, send_sem, recv_sem, back_send, back_recv):
    me = lax.axis_index("blk")
    column = lax.axis_index("head")
    barrier = pltpu.get_barrier_semaphore()
    for k in range(1, count):
        pl.semaphore_signal(
            barrier, 1, device_id=(lax.rem(me + k, count), column), device_id_type=MESH
        )
    pl.semaphore_wait(barrier, count - 1)
    outgoing = []
    for k in range(1, count):
        peer = lax.rem(me + k, count)
        copy = pltpu.make_async_remote_copy(
            src_ref=x_ref.at[peer],
            dst_ref=inbox.at[me],
            send_sem=send_sem.at[k],
            recv_sem=recv_sem.at[me],
            device_id=(peer, column),
            device_id_type=MESH,
        )
        copy.start()
        outgoing.append(copy)
    total = x_ref[me].astype(jnp.float32)
    for k in range(1, count):
        source = lax.rem(me + count - k, count)
        pltpu.make_async_remote_copy(
            src_ref=x_ref.at[source],
            dst_ref=inbox.at[source],
            send_sem=send_sem.at[k],
            recv_sem=recv_sem.at[source],
            device_id=(source, column),
            device_id_type=MESH,
        ).wait_recv()
        total = total + inbox[source].astype(jnp.float32)
    mine[...] = total.astype(mine.dtype)
    for k in range(1, count):
        peer = lax.rem(me + k, count)
        copy = pltpu.make_async_remote_copy(
            src_ref=mine,
            dst_ref=gathered.at[me],
            send_sem=back_send.at[k],
            recv_sem=back_recv.at[me],
            device_id=(peer, column),
            device_id_type=MESH,
        )
        copy.start()
        outgoing.append(copy)
    gathered[me] = mine[...]
    for k in range(1, count):
        source = lax.rem(me + count - k, count)
        pltpu.make_async_remote_copy(
            src_ref=mine,
            dst_ref=gathered.at[source],
            send_sem=back_send.at[k],
            recv_sem=back_recv.at[source],
            device_id=(source, column),
            device_id_type=MESH,
        ).wait_recv()
    for copy in outgoing:
        copy.wait_send()
    out_ref[...] = gathered[...]


def butterfly_sum(block, axis, collective):
    count = lax.axis_size(axis)
    if block.size % (count * 8 * 128):
        return lax.psum(block, axis)
    pieces = block.reshape(count, -1, 128)
    vmem = pltpu.VMEM
    summed = pl.pallas_call(
        functools.partial(reduce_kernel, count),
        out_shape=jax.ShapeDtypeStruct(pieces.shape, pieces.dtype),
        in_specs=[pl.BlockSpec(memory_space=vmem)],
        out_specs=pl.BlockSpec(memory_space=vmem),
        scratch_shapes=[
            pltpu.VMEM(pieces.shape, pieces.dtype),
            pltpu.VMEM(pieces.shape, pieces.dtype),
            pltpu.VMEM(pieces.shape[1:], pieces.dtype),
            pltpu.SemaphoreType.DMA((count,)),
            pltpu.SemaphoreType.DMA((count,)),
            pltpu.SemaphoreType.DMA((count,)),
            pltpu.SemaphoreType.DMA((count,)),
        ],
        compiler_params=pltpu.CompilerParams(collective_id=collective, has_side_effects=True),
    )(pieces)
    return summed.reshape(block.shape)


def swap_kernel(count, x_ref, down_ref, up_ref, out_ref, above_ref, below_ref, *scratch):
    inbox, gathered, mine, send_sem, recv_sem, back_send, back_recv = scratch[:7]
    from_above, from_below, near_send, near_recv = scratch[7:]
    me = lax.axis_index("blk")
    column = lax.axis_index("head")
    barrier = pltpu.get_barrier_semaphore()
    for k in range(1, count):
        pl.semaphore_signal(
            barrier, 1, device_id=(lax.rem(me + k, count), column), device_id_type=MESH
        )
    pl.semaphore_wait(barrier, count - 1)

    def downward():
        return pltpu.make_async_remote_copy(
            src_ref=down_ref,
            dst_ref=from_above,
            send_sem=near_send.at[0],
            recv_sem=near_recv.at[0],
            device_id=(me - 1, column),
            device_id_type=MESH,
        )

    def upward():
        return pltpu.make_async_remote_copy(
            src_ref=up_ref,
            dst_ref=from_below,
            send_sem=near_send.at[1],
            recv_sem=near_recv.at[1],
            device_id=(me + 1, column),
            device_id_type=MESH,
        )

    @pl.when(me > 0)
    def _():
        downward().start()

    @pl.when(me < count - 1)
    def _():
        upward().start()

    outgoing = []
    for k in range(1, count):
        peer = lax.rem(me + k, count)
        copy = pltpu.make_async_remote_copy(
            src_ref=x_ref.at[peer],
            dst_ref=inbox.at[me],
            send_sem=send_sem.at[k],
            recv_sem=recv_sem.at[me],
            device_id=(peer, column),
            device_id_type=MESH,
        )
        copy.start()
        outgoing.append(copy)
    total = x_ref[me].astype(jnp.float32)
    for k in range(1, count):
        source = lax.rem(me + count - k, count)
        pltpu.make_async_remote_copy(
            src_ref=x_ref.at[source],
            dst_ref=inbox.at[source],
            send_sem=send_sem.at[k],
            recv_sem=recv_sem.at[source],
            device_id=(source, column),
            device_id_type=MESH,
        ).wait_recv()
        total = total + inbox[source].astype(jnp.float32)
    mine[...] = total.astype(mine.dtype)
    for k in range(1, count):
        peer = lax.rem(me + k, count)
        copy = pltpu.make_async_remote_copy(
            src_ref=mine,
            dst_ref=gathered.at[me],
            send_sem=back_send.at[k],
            recv_sem=back_recv.at[me],
            device_id=(peer, column),
            device_id_type=MESH,
        )
        copy.start()
        outgoing.append(copy)
    gathered[me] = mine[...]
    for k in range(1, count):
        source = lax.rem(me + count - k, count)
        pltpu.make_async_remote_copy(
            src_ref=mine,
            dst_ref=gathered.at[source],
            send_sem=back_send.at[k],
            recv_sem=back_recv.at[source],
            device_id=(source, column),
            device_id_type=MESH,
        ).wait_recv()
    for copy in outgoing:
        copy.wait_send()
    out_ref[...] = gathered[...]

    @pl.when(me > 0)
    def _():
        downward().wait_send()
        upward().wait_recv()
        below_ref[...] = from_below[...]

    @pl.when(me == 0)
    def _():
        below_ref[...] = jnp.zeros_like(below_ref)

    @pl.when(me < count - 1)
    def _():
        upward().wait_send()
        downward().wait_recv()
        above_ref[...] = from_above[...]

    @pl.when(me == count - 1)
    def _():
        above_ref[...] = jnp.zeros_like(above_ref)


def sum_and_swap(block, down, up, axis, collective):
    count = lax.axis_size(axis)
    pieces = block.reshape(count, -1, 128)
    vmem = pltpu.VMEM
    summed, above, below = pl.pallas_call(
        functools.partial(swap_kernel, count),
        out_shape=(
            jax.ShapeDtypeStruct(pieces.shape, pieces.dtype),
            jax.ShapeDtypeStruct(down.shape, down.dtype),
            jax.ShapeDtypeStruct(up.shape, up.dtype),
        ),
        in_specs=[pl.BlockSpec(memory_space=vmem)] * 3,
        out_specs=tuple(pl.BlockSpec(memory_space=vmem) for _ in range(3)),
        scratch_shapes=[
            pltpu.VMEM(pieces.shape, pieces.dtype),
            pltpu.VMEM(pieces.shape, pieces.dtype),
            pltpu.VMEM(pieces.shape[1:], pieces.dtype),
            pltpu.SemaphoreType.DMA((count,)),
            pltpu.SemaphoreType.DMA((count,)),
            pltpu.SemaphoreType.DMA((count,)),
            pltpu.SemaphoreType.DMA((count,)),
            pltpu.VMEM(down.shape, down.dtype),
            pltpu.VMEM(up.shape, up.dtype),
            pltpu.SemaphoreType.DMA((2,)),
            pltpu.SemaphoreType.DMA((2,)),
        ],
        compiler_params=pltpu.CompilerParams(
            collective_id=collective, has_side_effects=True, vmem_limit_bytes=48 * 1024 * 1024
        ),
    )(pieces, down, up)
    return summed.reshape(block.shape), above, below


def split_heads(field, count):
    heads = field.shape[1] // HD
    return field.reshape(count, TILE, heads, HD).transpose(2, 0, 1, 3)


def merge_heads(field):
    heads = field.shape[0]
    count = field.shape[1]
    return field.transpose(1, 2, 0, 3).reshape(count * TILE, heads * HD)


def attention_kernel(index_ref, q_ref, do_ref, k_ref, v_ref, att_ref, dq_ref, dk_ref, dv_ref, kbuf, vbuf):
    heads = q_ref.shape[1] // HD
    tiles = q_ref.shape[0] // TILE
    slots = index_ref.shape[0] // (heads * tiles)
    scale = HD ** (-0.5)
    dk_ref[...] = jnp.zeros_like(dk_ref)
    dv_ref[...] = jnp.zeros_like(dv_ref)
    nt = (((1,), (1,)), ((), ()))
    tn = (((0,), (0,)), ((), ()))

    def step(item, carry):
        head = item // tiles
        tile = item % tiles
        cols = pl.ds(pl.multiple_of(head * HD, HD), HD)
        rows = pl.ds(pl.multiple_of(tile * TILE, TILE), TILE)
        picks = [
            pl.ds(pl.multiple_of(index_ref[item * slots + s] * TILE, TILE), TILE)
            for s in range(slots)
        ]
        for s in range(slots):
            kbuf[s * TILE : (s + 1) * TILE, :] = k_ref[picks[s], cols]
            vbuf[s * TILE : (s + 1) * TILE, :] = v_ref[picks[s], cols]
        query = q_ref[rows, cols]
        grad_out = do_ref[rows, cols]
        chosen_keys = kbuf[...]
        chosen_values = vbuf[...]
        scores = (
            lax.dot_general(query, chosen_keys, nt, preferred_element_type=jnp.float32) * scale
        )
        peak = jnp.max(scores, axis=1, keepdims=True)
        log_total = peak + jnp.log(jnp.sum(jnp.exp(scores - peak), axis=1, keepdims=True))
        probs = jnp.exp(scores - log_total)
        weights = probs.astype(jnp.bfloat16)
        attended = jnp.dot(weights, chosen_values, preferred_element_type=jnp.float32).astype(
            jnp.bfloat16
        )
        att_ref[rows, cols] = attended
        delta = jnp.sum(
            grad_out.astype(jnp.float32) * attended.astype(jnp.float32), axis=1, keepdims=True
        )
        grad_probs = lax.dot_general(
            grad_out, chosen_values, nt, preferred_element_type=jnp.float32
        )
        grad_scores = (probs * (grad_probs - delta)).astype(jnp.bfloat16)
        dq_ref[rows, cols] = (
            jnp.dot(grad_scores, chosen_keys, preferred_element_type=jnp.float32) * scale
        ).astype(jnp.bfloat16)
        key_slots = (
            lax.dot_general(grad_scores, query, tn, preferred_element_type=jnp.float32) * scale
        )
        value_slots = lax.dot_general(weights, grad_out, tn, preferred_element_type=jnp.float32)
        for s in range(slots):
            dk_ref[picks[s], cols] += key_slots[s * TILE : (s + 1) * TILE]
            dv_ref[picks[s], cols] += value_slots[s * TILE : (s + 1) * TILE]
        return carry

    lax.fori_loop(0, heads * tiles, step, 0)


def attend(pool_index, query_rows, grad_rows, pool_keys, pool_values):
    count, width = query_rows.shape
    pool_rows = pool_keys.shape[0]
    slots = pool_index.shape[-1]
    vmem = pltpu.VMEM
    flops = 2 * 7 * count * slots * TILE * width
    return pl.pallas_call(
        attention_kernel,
        out_shape=(
            jax.ShapeDtypeStruct((count, width), jnp.bfloat16),
            jax.ShapeDtypeStruct((count, width), jnp.bfloat16),
            jax.ShapeDtypeStruct((pool_rows, width), jnp.float32),
            jax.ShapeDtypeStruct((pool_rows, width), jnp.float32),
        ),
        in_specs=[pl.BlockSpec(memory_space=pltpu.SMEM)] + [pl.BlockSpec(memory_space=vmem)] * 4,
        out_specs=tuple(pl.BlockSpec(memory_space=vmem) for _ in range(4)),
        scratch_shapes=[
            pltpu.VMEM((slots * TILE, HD), jnp.bfloat16),
            pltpu.VMEM((slots * TILE, HD), jnp.bfloat16),
        ],
        compiler_params=pltpu.CompilerParams(vmem_limit_bytes=60 * 1024 * 1024),
        cost_estimate=pl.CostEstimate(
            flops=flops,
            transcendentals=count * slots * TILE * width // HD,
            bytes_accessed=8 * count * width + 12 * pool_rows * width,
        ),
    )(pool_index.reshape(-1), query_rows, grad_rows, pool_keys, pool_values)


def per_device(query, keys, values, cotangent, kv_tiles):
    head_count = lax.axis_size("head")
    cycle_pos = lax.axis_index("blk")
    per_frame = query.shape[0] * head_count // TILE
    reach = -(-HALF // per_frame)
    span = (2 * reach + 1) * per_frame
    global_tiles = kv_tiles[:, 0, :GLOBALS]
    own_tiles = lax.dynamic_slice_in_dim(kv_tiles, cycle_pos * per_frame, per_frame, 1)
    moved = lax.all_to_all(
        jnp.stack([query, keys, values, cotangent]), "head", split_axis=2, concat_axis=1, tiled=True
    )
    frame_keys = moved[1]
    frame_values = moved[2]
    offset = 1
    earlier = passed_along((frame_keys, frame_values), "blk", offset)
    later = passed_along((frame_keys, frame_values), "blk", -offset)
    earlier_keys = [earlier[0]]
    earlier_values = [earlier[1]]
    later_keys = [later[0]]
    later_values = [later[1]]
    near_keys = jnp.stack(earlier_keys[::-1] + later_keys, axis=0)
    near_values = jnp.stack(earlier_values[::-1] + later_values, axis=0)
    width = frame_keys.shape[1]
    all_keys = jnp.concatenate(
        [near_keys[:reach], frame_keys[None], near_keys[reach:]], axis=0
    ).reshape(span * TILE, width)
    all_values = jnp.concatenate(
        [near_values[:reach], frame_values[None], near_values[reach:]], axis=0
    ).reshape(span * TILE, width)
    heads = width // HD
    tile_ids = cycle_pos * per_frame + jnp.arange(per_frame, dtype=jnp.int32)
    owner = global_tiles[:, :, None] == tile_ids[None, None, :]
    owner_mask = owner.astype(jnp.bfloat16)
    frame_key_tiles = frame_keys.reshape(per_frame, TILE, heads, HD)
    frame_value_tiles = frame_values.reshape(per_frame, TILE, heads, HD)
    global_keys = jnp.einsum(
        "hjt,tkhd->jkhd", owner_mask, frame_key_tiles, preferred_element_type=jnp.float32
    )
    global_values = jnp.einsum(
        "hjt,tkhd->jkhd", owner_mask, frame_value_tiles, preferred_element_type=jnp.float32
    )
    global_both = butterfly_sum(
        jnp.stack([global_keys.astype(jnp.bfloat16), global_values.astype(jnp.bfloat16)]), "blk", 0
    )
    global_rows = GLOBALS * TILE
    pool_keys = jnp.concatenate([all_keys, global_both[0].reshape(global_rows, width)], axis=0)
    pool_values = jnp.concatenate([all_values, global_both[1].reshape(global_rows, width)], axis=0)
    relative = own_tiles - (cycle_pos - reach) * per_frame
    inside = (relative >= 0) & (relative < span)
    matches = own_tiles[:, :, :, None] == global_tiles[:, None, None, :]
    slot_numbers = jnp.arange(global_tiles.shape[1], dtype=jnp.int32)
    global_slot = jnp.sum(jnp.where(matches, slot_numbers[None, None, None, :], 0), axis=-1)
    pool_index = jnp.where(inside, relative, span + global_slot)
    attended, query_rows, key_pool, value_pool = attend(
        pool_index, moved[0], moved[3], pool_keys, pool_values
    )
    frame_rows = per_frame * TILE
    centre = reach * frame_rows
    key_grad = key_pool[centre : centre + frame_rows]
    value_grad = value_pool[centre : centre + frame_rows]
    lower = (reach - 1) * frame_rows
    upper = (reach + 1) * frame_rows
    down = jnp.stack([key_pool[lower : lower + frame_rows], value_pool[lower : lower + frame_rows]])
    up = jnp.stack([key_pool[upper : upper + frame_rows], value_pool[upper : upper + frame_rows]])
    pool_end = span * TILE
    summed, above, below = sum_and_swap(
        jnp.stack([key_pool[pool_end:], value_pool[pool_end:]]).reshape(
            2, GLOBALS, TILE, heads, HD
        ),
        down.astype(jnp.bfloat16),
        up.astype(jnp.bfloat16),
        "blk",
        1,
    )
    returned = above.astype(jnp.float32) + below.astype(jnp.float32)
    key_grad = key_grad + returned[0]
    value_grad = value_grad + returned[1]
    owner_float = owner.astype(jnp.float32)
    key_grad = key_grad + jnp.einsum(
        "hjt,jkhd->tkhd", owner_float, summed[0], precision=lax.Precision.HIGHEST
    ).reshape(frame_rows, width)
    value_grad = value_grad + jnp.einsum(
        "hjt,jkhd->tkhd", owner_float, summed[1], precision=lax.Precision.HIGHEST
    ).reshape(frame_rows, width)
    key_rows = key_grad.astype(jnp.bfloat16)
    value_rows = value_grad.astype(jnp.bfloat16)
    forward_back = lax.all_to_all(
        jnp.stack([attended, query_rows]), "head", split_axis=1, concat_axis=2, tiled=True
    )
    backward_back = lax.all_to_all(
        jnp.stack([key_rows, value_rows]), "head", split_axis=1, concat_axis=2, tiled=True
    )
    results = (forward_back[0], forward_back[1], backward_back[0], backward_back[1])
    return (results[0], results[1], results[2], results[3])


def solution(mesh):
    placed = (
        P(("blk", "head"), None),
        P(("blk", "head"), None),
        P(("blk", "head"), None),
        P(("blk", "head"), None),
        P("head", None, None),
    )
    return jax.shard_map(
        per_device,
        mesh=mesh,
        in_specs=placed,
        out_specs=(
            P(("blk", "head"), None),
            P(("blk", "head"), None),
            P(("blk", "head"), None),
            P(("blk", "head"), None),
        ),
        check_vma=False,
    )
```

```python
import functools

import jax
import jax.numpy as jnp
from jax import lax
from jax.experimental import pallas as pl
from jax.experimental.pallas import tpu as pltpu
from jax.sharding import PartitionSpec as P

MESH = pl.DeviceIdType.MESH
HD = 128
TILE = 128
GLOBALS = 2
HALF = 8


def passed_along(block, axis, distance):
    devices = range(lax.axis_size(axis))
    route = [(i - distance, i) for i in devices if i - distance in devices]
    return lax.ppermute(block, axis, route)


def reduce_kernel(count, x_ref, out_ref, inbox, gathered, mine, send_sem, recv_sem, back_send, back_recv):
    me = lax.axis_index("blk")
    column = lax.axis_index("head")
    barrier = pltpu.get_barrier_semaphore()
    for k in range(1, count):
        pl.semaphore_signal(
            barrier, 1, device_id=(lax.rem(me + k, count), column), device_id_type=MESH
        )
    pl.semaphore_wait(barrier, count - 1)
    outgoing = []
    for k in range(1, count):
        peer = lax.rem(me + k, count)
        copy = pltpu.make_async_remote_copy(
            src_ref=x_ref.at[peer],
            dst_ref=inbox.at[me],
            send_sem=send_sem.at[k],
            recv_sem=recv_sem.at[me],
            device_id=(peer, column),
            device_id_type=MESH,
        )
        copy.start()
        outgoing.append(copy)
    total = x_ref[me].astype(jnp.float32)
    for k in range(1, count):
        source = lax.rem(me + count - k, count)
        pltpu.make_async_remote_copy(
            src_ref=x_ref.at[source],
            dst_ref=inbox.at[source],
            send_sem=send_sem.at[k],
            recv_sem=recv_sem.at[source],
            device_id=(source, column),
            device_id_type=MESH,
        ).wait_recv()
        total = total + inbox[source].astype(jnp.float32)
    mine[...] = total.astype(mine.dtype)
    for k in range(1, count):
        peer = lax.rem(me + k, count)
        copy = pltpu.make_async_remote_copy(
            src_ref=mine,
            dst_ref=gathered.at[me],
            send_sem=back_send.at[k],
            recv_sem=back_recv.at[me],
            device_id=(peer, column),
            device_id_type=MESH,
        )
        copy.start()
        outgoing.append(copy)
    gathered[me] = mine[...]
    for k in range(1, count):
        source = lax.rem(me + count - k, count)
        pltpu.make_async_remote_copy(
            src_ref=mine,
            dst_ref=gathered.at[source],
            send_sem=back_send.at[k],
            recv_sem=back_recv.at[source],
            device_id=(source, column),
            device_id_type=MESH,
        ).wait_recv()
    for copy in outgoing:
        copy.wait_send()
    out_ref[...] = gathered[...]


def butterfly_sum(block, axis, collective):
    count = lax.axis_size(axis)
    if block.size % (count * 8 * 128):
        return lax.psum(block, axis)
    pieces = block.reshape(count, -1, 128)
    vmem = pltpu.VMEM
    summed = pl.pallas_call(
        functools.partial(reduce_kernel, count),
        out_shape=jax.ShapeDtypeStruct(pieces.shape, pieces.dtype),
        in_specs=[pl.BlockSpec(memory_space=vmem)],
        out_specs=pl.BlockSpec(memory_space=vmem),
        scratch_shapes=[
            pltpu.VMEM(pieces.shape, pieces.dtype),
            pltpu.VMEM(pieces.shape, pieces.dtype),
            pltpu.VMEM(pieces.shape[1:], pieces.dtype),
            pltpu.SemaphoreType.DMA((count,)),
            pltpu.SemaphoreType.DMA((count,)),
            pltpu.SemaphoreType.DMA((count,)),
            pltpu.SemaphoreType.DMA((count,)),
        ],
        compiler_params=pltpu.CompilerParams(collective_id=collective, has_side_effects=True),
    )(pieces)
    return summed.reshape(block.shape)


def split_heads(field, count):
    heads = field.shape[1] // HD
    return field.reshape(count, TILE, heads, HD).transpose(2, 0, 1, 3)


def merge_heads(field):
    heads = field.shape[0]
    count = field.shape[1]
    return field.transpose(1, 2, 0, 3).reshape(count * TILE, heads * HD)


def attention_kernel(index_ref, q_ref, do_ref, k_ref, v_ref, att_ref, dq_ref, dk_ref, dv_ref, kbuf, vbuf):
    heads = q_ref.shape[1] // HD
    tiles = q_ref.shape[0] // TILE
    slots = index_ref.shape[0] // (heads * tiles)
    scale = HD ** (-0.5)
    dk_ref[...] = jnp.zeros_like(dk_ref)
    dv_ref[...] = jnp.zeros_like(dv_ref)
    nt = (((1,), (1,)), ((), ()))
    tn = (((0,), (0,)), ((), ()))

    def step(item, carry):
        head = item // tiles
        tile = item % tiles
        cols = pl.ds(pl.multiple_of(head * HD, HD), HD)
        rows = pl.ds(pl.multiple_of(tile * TILE, TILE), TILE)
        picks = [
            pl.ds(pl.multiple_of(index_ref[item * slots + s] * TILE, TILE), TILE)
            for s in range(slots)
        ]
        for s in range(slots):
            kbuf[s * TILE : (s + 1) * TILE, :] = k_ref[picks[s], cols]
            vbuf[s * TILE : (s + 1) * TILE, :] = v_ref[picks[s], cols]
        query = q_ref[rows, cols]
        grad_out = do_ref[rows, cols]
        chosen_keys = kbuf[...]
        chosen_values = vbuf[...]
        scores = (
            lax.dot_general(query, chosen_keys, nt, preferred_element_type=jnp.float32) * scale
        )
        peak = jnp.max(scores, axis=1, keepdims=True)
        lifted = jnp.exp(scores - peak)
        probs = lifted * (1.0 / jnp.sum(lifted, axis=1, keepdims=True))
        weights = probs.astype(jnp.bfloat16)
        attended = jnp.dot(weights, chosen_values, preferred_element_type=jnp.float32).astype(
            jnp.bfloat16
        )
        att_ref[rows, cols] = attended
        delta = jnp.sum(
            grad_out.astype(jnp.float32) * attended.astype(jnp.float32), axis=1, keepdims=True
        )
        grad_probs = lax.dot_general(
            grad_out, chosen_values, nt, preferred_element_type=jnp.float32
        )
        grad_scores = (probs * (grad_probs - delta)).astype(jnp.bfloat16)
        dq_ref[rows, cols] = (
            jnp.dot(grad_scores, chosen_keys, preferred_element_type=jnp.float32) * scale
        ).astype(jnp.bfloat16)
        key_slots = (
            lax.dot_general(grad_scores, query, tn, preferred_element_type=jnp.float32) * scale
        )
        value_slots = lax.dot_general(weights, grad_out, tn, preferred_element_type=jnp.float32)
        for s in range(slots):
            dk_ref[picks[s], cols] += key_slots[s * TILE : (s + 1) * TILE]
            dv_ref[picks[s], cols] += value_slots[s * TILE : (s + 1) * TILE]
        return carry

    lax.fori_loop(0, heads * tiles, step, 0)


def attend(pool_index, query_rows, grad_rows, pool_keys, pool_values):
    count, width = query_rows.shape
    pool_rows = pool_keys.shape[0]
    slots = pool_index.shape[-1]
    vmem = pltpu.VMEM
    flops = 2 * 7 * count * slots * TILE * width
    return pl.pallas_call(
        attention_kernel,
        out_shape=(
            jax.ShapeDtypeStruct((count, width), jnp.bfloat16),
            jax.ShapeDtypeStruct((count, width), jnp.bfloat16),
            jax.ShapeDtypeStruct((pool_rows, width), jnp.float32),
            jax.ShapeDtypeStruct((pool_rows, width), jnp.float32),
        ),
        in_specs=[pl.BlockSpec(memory_space=pltpu.SMEM)] + [pl.BlockSpec(memory_space=vmem)] * 4,
        out_specs=tuple(pl.BlockSpec(memory_space=vmem) for _ in range(4)),
        scratch_shapes=[
            pltpu.VMEM((slots * TILE, HD), jnp.bfloat16),
            pltpu.VMEM((slots * TILE, HD), jnp.bfloat16),
        ],
        compiler_params=pltpu.CompilerParams(vmem_limit_bytes=60 * 1024 * 1024),
        cost_estimate=pl.CostEstimate(
            flops=flops,
            transcendentals=count * slots * TILE * width // HD,
            bytes_accessed=8 * count * width + 12 * pool_rows * width,
        ),
    )(pool_index.reshape(-1), query_rows, grad_rows, pool_keys, pool_values)


def per_device(query, keys, values, cotangent, kv_tiles):
    head_count = lax.axis_size("head")
    cycle_pos = lax.axis_index("blk")
    per_frame = query.shape[0] * head_count // TILE
    reach = -(-HALF // per_frame)
    span = (2 * reach + 1) * per_frame
    global_tiles = kv_tiles[:, 0, :GLOBALS]
    own_tiles = lax.dynamic_slice_in_dim(kv_tiles, cycle_pos * per_frame, per_frame, 1)
    moved = lax.all_to_all(
        jnp.stack([query, keys, values, cotangent]), "head", split_axis=2, concat_axis=1, tiled=True
    )
    frame_keys = moved[1]
    frame_values = moved[2]
    offset = 1
    earlier = passed_along((frame_keys, frame_values), "blk", offset)
    later = passed_along((frame_keys, frame_values), "blk", -offset)
    earlier_keys = [earlier[0]]
    earlier_values = [earlier[1]]
    later_keys = [later[0]]
    later_values = [later[1]]
    near_keys = jnp.stack(earlier_keys[::-1] + later_keys, axis=0)
    near_values = jnp.stack(earlier_values[::-1] + later_values, axis=0)
    width = frame_keys.shape[1]
    all_keys = jnp.concatenate(
        [near_keys[:reach], frame_keys[None], near_keys[reach:]], axis=0
    ).reshape(span * TILE, width)
    all_values = jnp.concatenate(
        [near_values[:reach], frame_values[None], near_values[reach:]], axis=0
    ).reshape(span * TILE, width)
    heads = width // HD
    tile_ids = cycle_pos * per_frame + jnp.arange(per_frame, dtype=jnp.int32)
    owner = global_tiles[:, :, None] == tile_ids[None, None, :]
    owner_mask = owner.astype(jnp.bfloat16)
    frame_key_tiles = frame_keys.reshape(per_frame, TILE, heads, HD)
    frame_value_tiles = frame_values.reshape(per_frame, TILE, heads, HD)
    global_keys = jnp.einsum(
        "hjt,tkhd->jkhd", owner_mask, frame_key_tiles, preferred_element_type=jnp.float32
    )
    global_values = jnp.einsum(
        "hjt,tkhd->jkhd", owner_mask, frame_value_tiles, preferred_element_type=jnp.float32
    )
    global_both = butterfly_sum(
        jnp.stack([global_keys.astype(jnp.bfloat16), global_values.astype(jnp.bfloat16)]), "blk", 0
    )
    global_rows = GLOBALS * TILE
    pool_keys = jnp.concatenate([all_keys, global_both[0].reshape(global_rows, width)], axis=0)
    pool_values = jnp.concatenate([all_values, global_both[1].reshape(global_rows, width)], axis=0)
    relative = own_tiles - (cycle_pos - reach) * per_frame
    inside = (relative >= 0) & (relative < span)
    matches = own_tiles[:, :, :, None] == global_tiles[:, None, None, :]
    slot_numbers = jnp.arange(global_tiles.shape[1], dtype=jnp.int32)
    global_slot = jnp.sum(jnp.where(matches, slot_numbers[None, None, None, :], 0), axis=-1)
    pool_index = jnp.where(inside, relative, span + global_slot)
    attended, query_rows, key_pool, value_pool = attend(
        pool_index, moved[0], moved[3], pool_keys, pool_values
    )
    frame_rows = per_frame * TILE
    centre = reach * frame_rows
    key_grad = key_pool[centre : centre + frame_rows]
    value_grad = value_pool[centre : centre + frame_rows]
    offset = 1
    lower = (reach - offset) * frame_rows
    returned = (
        passed_along(
            key_pool[lower : lower + frame_rows].astype(jnp.bfloat16), "blk", -offset
        ).astype(jnp.float32),
        passed_along(
            value_pool[lower : lower + frame_rows].astype(jnp.bfloat16), "blk", -offset
        ).astype(jnp.float32),
    )
    key_grad = key_grad + returned[0]
    value_grad = value_grad + returned[1]
    upper = (reach + offset) * frame_rows
    returned = (
        passed_along(
            key_pool[upper : upper + frame_rows].astype(jnp.bfloat16), "blk", offset
        ).astype(jnp.float32),
        passed_along(
            value_pool[upper : upper + frame_rows].astype(jnp.bfloat16), "blk", offset
        ).astype(jnp.float32),
    )
    key_grad = key_grad + returned[0]
    value_grad = value_grad + returned[1]
    pool_end = span * TILE
    summed = butterfly_sum(
        jnp.stack([key_pool[pool_end:], value_pool[pool_end:]]).reshape(
            2, GLOBALS, TILE, heads, HD
        ),
        "blk",
        1,
    )
    owner_float = owner.astype(jnp.float32)
    key_grad = key_grad + jnp.einsum(
        "hjt,jkhd->tkhd", owner_float, summed[0], precision=lax.Precision.HIGHEST
    ).reshape(frame_rows, width)
    value_grad = value_grad + jnp.einsum(
        "hjt,jkhd->tkhd", owner_float, summed[1], precision=lax.Precision.HIGHEST
    ).reshape(frame_rows, width)
    key_rows = key_grad.astype(jnp.bfloat16)
    value_rows = value_grad.astype(jnp.bfloat16)
    forward_back = lax.all_to_all(
        jnp.stack([attended, query_rows]), "head", split_axis=1, concat_axis=2, tiled=True
    )
    backward_back = lax.all_to_all(
        jnp.stack([key_rows, value_rows]), "head", split_axis=1, concat_axis=2, tiled=True
    )
    results = (forward_back[0], forward_back[1], backward_back[0], backward_back[1])
    return (results[0], results[1], results[2], results[3])


def solution(mesh):
    placed = (
        P(("blk", "head"), None),
        P(("blk", "head"), None),
        P(("blk", "head"), None),
        P(("blk", "head"), None),
        P("head", None, None),
    )
    return jax.shard_map(
        per_device,
        mesh=mesh,
        in_specs=placed,
        out_specs=(
            P(("blk", "head"), None),
            P(("blk", "head"), None),
            P(("blk", "head"), None),
            P(("blk", "head"), None),
        ),
        check_vma=False,
    )
```

```python
import functools

import jax
import jax.numpy as jnp
from jax import lax
from jax.experimental import pallas as pl
from jax.experimental.pallas import tpu as pltpu
from jax.sharding import PartitionSpec as P

MESH = pl.DeviceIdType.MESH
HD = 128
TILE = 128
GLOBALS = 2
HALF = 8


def passed_along(block, axis, distance):
    devices = range(lax.axis_size(axis))
    route = [(i - distance, i) for i in devices if i - distance in devices]
    return lax.ppermute(block, axis, route)


def reduce_kernel(count, x_ref, out_ref, inbox, gathered, mine, send_sem, recv_sem, back_send, back_recv):
    me = lax.axis_index("blk")
    column = lax.axis_index("head")
    barrier = pltpu.get_barrier_semaphore()
    for k in range(1, count):
        pl.semaphore_signal(
            barrier, 1, device_id=(lax.rem(me + k, count), column), device_id_type=MESH
        )
    pl.semaphore_wait(barrier, count - 1)
    outgoing = []
    for k in range(1, count):
        peer = lax.rem(me + k, count)
        copy = pltpu.make_async_remote_copy(
            src_ref=x_ref.at[peer],
            dst_ref=inbox.at[me],
            send_sem=send_sem.at[k],
            recv_sem=recv_sem.at[me],
            device_id=(peer, column),
            device_id_type=MESH,
        )
        copy.start()
        outgoing.append(copy)
    total = x_ref[me].astype(jnp.float32)
    for k in range(1, count):
        source = lax.rem(me + count - k, count)
        pltpu.make_async_remote_copy(
            src_ref=x_ref.at[source],
            dst_ref=inbox.at[source],
            send_sem=send_sem.at[k],
            recv_sem=recv_sem.at[source],
            device_id=(source, column),
            device_id_type=MESH,
        ).wait_recv()
        total = total + inbox[source].astype(jnp.float32)
    mine[...] = total.astype(mine.dtype)
    for k in range(1, count):
        peer = lax.rem(me + k, count)
        copy = pltpu.make_async_remote_copy(
            src_ref=mine,
            dst_ref=gathered.at[me],
            send_sem=back_send.at[k],
            recv_sem=back_recv.at[me],
            device_id=(peer, column),
            device_id_type=MESH,
        )
        copy.start()
        outgoing.append(copy)
    gathered[me] = mine[...]
    for k in range(1, count):
        source = lax.rem(me + count - k, count)
        pltpu.make_async_remote_copy(
            src_ref=mine,
            dst_ref=gathered.at[source],
            send_sem=back_send.at[k],
            recv_sem=back_recv.at[source],
            device_id=(source, column),
            device_id_type=MESH,
        ).wait_recv()
    for copy in outgoing:
        copy.wait_send()
    out_ref[...] = gathered[...]


def butterfly_sum(block, axis, collective):
    count = lax.axis_size(axis)
    if block.size % (count * 8 * 128):
        return lax.psum(block, axis)
    pieces = block.reshape(count, -1, 128)
    vmem = pltpu.VMEM
    summed = pl.pallas_call(
        functools.partial(reduce_kernel, count),
        out_shape=jax.ShapeDtypeStruct(pieces.shape, pieces.dtype),
        in_specs=[pl.BlockSpec(memory_space=vmem)],
        out_specs=pl.BlockSpec(memory_space=vmem),
        scratch_shapes=[
            pltpu.VMEM(pieces.shape, pieces.dtype),
            pltpu.VMEM(pieces.shape, pieces.dtype),
            pltpu.VMEM(pieces.shape[1:], pieces.dtype),
            pltpu.SemaphoreType.DMA((count,)),
            pltpu.SemaphoreType.DMA((count,)),
            pltpu.SemaphoreType.DMA((count,)),
            pltpu.SemaphoreType.DMA((count,)),
        ],
        compiler_params=pltpu.CompilerParams(collective_id=collective, has_side_effects=True),
    )(pieces)
    return summed.reshape(block.shape)


def split_heads(field, count):
    heads = field.shape[1] // HD
    return field.reshape(count, TILE, heads, HD).transpose(2, 0, 1, 3)


def merge_heads(field):
    heads = field.shape[0]
    count = field.shape[1]
    return field.transpose(1, 2, 0, 3).reshape(count * TILE, heads * HD)


def attention_kernel(index_ref, q_ref, do_ref, k_ref, v_ref, att_ref, dq_ref, dk_ref, dv_ref, kbuf, vbuf):
    heads = q_ref.shape[1] // HD
    tiles = q_ref.shape[0] // TILE
    slots = index_ref.shape[0] // (heads * tiles)
    scale = HD ** (-0.5)
    dk_ref[...] = jnp.zeros_like(dk_ref)
    dv_ref[...] = jnp.zeros_like(dv_ref)
    nt = (((1,), (1,)), ((), ()))
    tn = (((0,), (0,)), ((), ()))

    def step(item, carry):
        head = item // tiles
        tile = item % tiles
        cols = pl.ds(pl.multiple_of(head * HD, HD), HD)
        rows = pl.ds(pl.multiple_of(tile * TILE, TILE), TILE)
        picks = [
            pl.ds(pl.multiple_of(index_ref[item * slots + s] * TILE, TILE), TILE)
            for s in range(slots)
        ]
        for s in range(slots):
            kbuf[s * TILE : (s + 1) * TILE, :] = k_ref[picks[s], cols]
            vbuf[s * TILE : (s + 1) * TILE, :] = v_ref[picks[s], cols]
        query = q_ref[rows, cols]
        grad_out = do_ref[rows, cols]
        chosen_keys = kbuf[...]
        chosen_values = vbuf[...]
        scores = (
            lax.dot_general(query, chosen_keys, nt, preferred_element_type=jnp.float32) * scale
        )
        peak = jnp.max(scores, axis=1, keepdims=True)
        log_total = peak + jnp.log(jnp.sum(jnp.exp(scores - peak), axis=1, keepdims=True))
        probs = jnp.exp(scores - log_total)
        weights = probs.astype(jnp.bfloat16)
        attended = jnp.dot(weights, chosen_values, preferred_element_type=jnp.float32).astype(
            jnp.bfloat16
        )
        att_ref[rows, cols] = attended
        delta = jnp.sum(
            grad_out.astype(jnp.float32) * attended.astype(jnp.float32), axis=1, keepdims=True
        )
        grad_probs = lax.dot_general(
            grad_out, chosen_values, nt, preferred_element_type=jnp.float32
        )
        grad_scores = (probs * (grad_probs - delta)).astype(jnp.bfloat16)
        dq_ref[rows, cols] = (
            jnp.dot(grad_scores, chosen_keys, preferred_element_type=jnp.float32) * scale
        ).astype(jnp.bfloat16)
        key_slots = (
            lax.dot_general(grad_scores, query, tn, preferred_element_type=jnp.float32) * scale
        )
        value_slots = lax.dot_general(weights, grad_out, tn, preferred_element_type=jnp.float32)
        for s in range(slots):
            dk_ref[picks[s], cols] += key_slots[s * TILE : (s + 1) * TILE]
            dv_ref[picks[s], cols] += value_slots[s * TILE : (s + 1) * TILE]
        return carry

    lax.fori_loop(0, heads * tiles, step, 0)


def attend(pool_index, query_rows, grad_rows, pool_keys, pool_values):
    count, width = query_rows.shape
    pool_rows = pool_keys.shape[0]
    slots = pool_index.shape[-1]
    vmem = pltpu.VMEM
    flops = 2 * 7 * count * slots * TILE * width
    return pl.pallas_call(
        attention_kernel,
        out_shape=(
            jax.ShapeDtypeStruct((count, width), jnp.bfloat16),
            jax.ShapeDtypeStruct((count, width), jnp.bfloat16),
            jax.ShapeDtypeStruct((pool_rows, width), jnp.float32),
            jax.ShapeDtypeStruct((pool_rows, width), jnp.float32),
        ),
        in_specs=[pl.BlockSpec(memory_space=pltpu.SMEM)] + [pl.BlockSpec(memory_space=vmem)] * 4,
        out_specs=tuple(pl.BlockSpec(memory_space=vmem) for _ in range(4)),
        scratch_shapes=[
            pltpu.VMEM((slots * TILE, HD), jnp.bfloat16),
            pltpu.VMEM((slots * TILE, HD), jnp.bfloat16),
        ],
        compiler_params=pltpu.CompilerParams(vmem_limit_bytes=60 * 1024 * 1024),
        cost_estimate=pl.CostEstimate(
            flops=flops,
            transcendentals=count * slots * TILE * width // HD,
            bytes_accessed=8 * count * width + 12 * pool_rows * width,
        ),
    )(pool_index.reshape(-1), query_rows, grad_rows, pool_keys, pool_values)


def per_device(query, keys, values, cotangent, kv_tiles):
    head_count = lax.axis_size("head")
    cycle_pos = lax.axis_index("blk")
    per_frame = query.shape[0] * head_count // TILE
    reach = -(-HALF // per_frame)
    span = (2 * reach + 1) * per_frame
    global_tiles = kv_tiles[:, 0, :GLOBALS]
    own_tiles = lax.dynamic_slice_in_dim(kv_tiles, cycle_pos * per_frame, per_frame, 1)
    moved_kv = lax.all_to_all(
        jnp.stack([keys, values]), "head", split_axis=2, concat_axis=1, tiled=True
    )
    moved_qg = lax.all_to_all(
        jnp.stack([query, cotangent]), "head", split_axis=2, concat_axis=1, tiled=True
    )
    moved = (moved_qg[0], moved_kv[0], moved_kv[1], moved_qg[1])
    frame_keys = moved[1]
    frame_values = moved[2]
    offset = 1
    earlier = passed_along((frame_keys, frame_values), "blk", offset)
    later = passed_along((frame_keys, frame_values), "blk", -offset)
    earlier_keys = [earlier[0]]
    earlier_values = [earlier[1]]
    later_keys = [later[0]]
    later_values = [later[1]]
    near_keys = jnp.stack(earlier_keys[::-1] + later_keys, axis=0)
    near_values = jnp.stack(earlier_values[::-1] + later_values, axis=0)
    width = frame_keys.shape[1]
    all_keys = jnp.concatenate(
        [near_keys[:reach], frame_keys[None], near_keys[reach:]], axis=0
    ).reshape(span * TILE, width)
    all_values = jnp.concatenate(
        [near_values[:reach], frame_values[None], near_values[reach:]], axis=0
    ).reshape(span * TILE, width)
    heads = width // HD
    tile_ids = cycle_pos * per_frame + jnp.arange(per_frame, dtype=jnp.int32)
    owner = global_tiles[:, :, None] == tile_ids[None, None, :]
    owner_mask = owner.astype(jnp.bfloat16)
    frame_key_tiles = frame_keys.reshape(per_frame, TILE, heads, HD)
    frame_value_tiles = frame_values.reshape(per_frame, TILE, heads, HD)
    global_keys = jnp.einsum(
        "hjt,tkhd->jkhd", owner_mask, frame_key_tiles, preferred_element_type=jnp.float32
    )
    global_values = jnp.einsum(
        "hjt,tkhd->jkhd", owner_mask, frame_value_tiles, preferred_element_type=jnp.float32
    )
    global_both = butterfly_sum(
        jnp.stack([global_keys.astype(jnp.bfloat16), global_values.astype(jnp.bfloat16)]), "blk", 0
    )
    global_rows = GLOBALS * TILE
    pool_keys = jnp.concatenate([all_keys, global_both[0].reshape(global_rows, width)], axis=0)
    pool_values = jnp.concatenate([all_values, global_both[1].reshape(global_rows, width)], axis=0)
    relative = own_tiles - (cycle_pos - reach) * per_frame
    inside = (relative >= 0) & (relative < span)
    matches = own_tiles[:, :, :, None] == global_tiles[:, None, None, :]
    slot_numbers = jnp.arange(global_tiles.shape[1], dtype=jnp.int32)
    global_slot = jnp.sum(jnp.where(matches, slot_numbers[None, None, None, :], 0), axis=-1)
    pool_index = jnp.where(inside, relative, span + global_slot)
    attended, query_rows, key_pool, value_pool = attend(
        pool_index, moved[0], moved[3], pool_keys, pool_values
    )
    frame_rows = per_frame * TILE
    centre = reach * frame_rows
    key_grad = key_pool[centre : centre + frame_rows]
    value_grad = value_pool[centre : centre + frame_rows]
    offset = 1
    lower = (reach - offset) * frame_rows
    returned = (
        passed_along(
            key_pool[lower : lower + frame_rows].astype(jnp.bfloat16), "blk", -offset
        ).astype(jnp.float32),
        passed_along(
            value_pool[lower : lower + frame_rows].astype(jnp.bfloat16), "blk", -offset
        ).astype(jnp.float32),
    )
    key_grad = key_grad + returned[0]
    value_grad = value_grad + returned[1]
    upper = (reach + offset) * frame_rows
    returned = (
        passed_along(
            key_pool[upper : upper + frame_rows].astype(jnp.bfloat16), "blk", offset
        ).astype(jnp.float32),
        passed_along(
            value_pool[upper : upper + frame_rows].astype(jnp.bfloat16), "blk", offset
        ).astype(jnp.float32),
    )
    key_grad = key_grad + returned[0]
    value_grad = value_grad + returned[1]
    pool_end = span * TILE
    summed = butterfly_sum(
        jnp.stack([key_pool[pool_end:], value_pool[pool_end:]]).reshape(
            2, GLOBALS, TILE, heads, HD
        ),
        "blk",
        1,
    )
    owner_float = owner.astype(jnp.float32)
    key_grad = key_grad + jnp.einsum(
        "hjt,jkhd->tkhd", owner_float, summed[0], precision=lax.Precision.HIGHEST
    ).reshape(frame_rows, width)
    value_grad = value_grad + jnp.einsum(
        "hjt,jkhd->tkhd", owner_float, summed[1], precision=lax.Precision.HIGHEST
    ).reshape(frame_rows, width)
    key_rows = key_grad.astype(jnp.bfloat16)
    value_rows = value_grad.astype(jnp.bfloat16)
    forward_back = lax.all_to_all(
        jnp.stack([attended, query_rows]), "head", split_axis=1, concat_axis=2, tiled=True
    )
    backward_back = lax.all_to_all(
        jnp.stack([key_rows, value_rows]), "head", split_axis=1, concat_axis=2, tiled=True
    )
    results = (forward_back[0], forward_back[1], backward_back[0], backward_back[1])
    return (results[0], results[1], results[2], results[3])


def solution(mesh):
    placed = (
        P(("blk", "head"), None),
        P(("blk", "head"), None),
        P(("blk", "head"), None),
        P(("blk", "head"), None),
        P("head", None, None),
    )
    return jax.shard_map(
        per_device,
        mesh=mesh,
        in_specs=placed,
        out_specs=(
            P(("blk", "head"), None),
            P(("blk", "head"), None),
            P(("blk", "head"), None),
            P(("blk", "head"), None),
        ),
        check_vma=False,
    )
```

```python
import functools

import jax
import jax.numpy as jnp
from jax import lax
from jax.experimental import pallas as pl
from jax.experimental.pallas import tpu as pltpu
from jax.sharding import PartitionSpec as P

MESH = pl.DeviceIdType.MESH
HD = 128
TILE = 128
GLOBALS = 2
HALF = 8


def passed_along(block, axis, distance):
    devices = range(lax.axis_size(axis))
    route = [(i - distance, i) for i in devices if i - distance in devices]
    return lax.ppermute(block, axis, route)


def reduce_kernel(count, x_ref, out_ref, inbox, gathered, mine, send_sem, recv_sem, back_send, back_recv):
    me = lax.axis_index("blk")
    column = lax.axis_index("head")
    barrier = pltpu.get_barrier_semaphore()
    for k in range(1, count):
        pl.semaphore_signal(
            barrier, 1, device_id=(lax.rem(me + k, count), column), device_id_type=MESH
        )
    pl.semaphore_wait(barrier, count - 1)
    outgoing = []
    for k in range(1, count):
        peer = lax.rem(me + k, count)
        copy = pltpu.make_async_remote_copy(
            src_ref=x_ref.at[peer],
            dst_ref=inbox.at[me],
            send_sem=send_sem.at[k],
            recv_sem=recv_sem.at[me],
            device_id=(peer, column),
            device_id_type=MESH,
        )
        copy.start()
        outgoing.append(copy)
    total = x_ref[me].astype(jnp.float32)
    for k in range(1, count):
        source = lax.rem(me + count - k, count)
        pltpu.make_async_remote_copy(
            src_ref=x_ref.at[source],
            dst_ref=inbox.at[source],
            send_sem=send_sem.at[k],
            recv_sem=recv_sem.at[source],
            device_id=(source, column),
            device_id_type=MESH,
        ).wait_recv()
        total = total + inbox[source].astype(jnp.float32)
    mine[...] = total.astype(mine.dtype)
    for k in range(1, count):
        peer = lax.rem(me + k, count)
        copy = pltpu.make_async_remote_copy(
            src_ref=mine,
            dst_ref=gathered.at[me],
            send_sem=back_send.at[k],
            recv_sem=back_recv.at[me],
            device_id=(peer, column),
            device_id_type=MESH,
        )
        copy.start()
        outgoing.append(copy)
    gathered[me] = mine[...]
    for k in range(1, count):
        source = lax.rem(me + count - k, count)
        pltpu.make_async_remote_copy(
            src_ref=mine,
            dst_ref=gathered.at[source],
            send_sem=back_send.at[k],
            recv_sem=back_recv.at[source],
            device_id=(source, column),
            device_id_type=MESH,
        ).wait_recv()
    for copy in outgoing:
        copy.wait_send()
    out_ref[...] = gathered[...]


def butterfly_sum(block, axis, collective):
    count = lax.axis_size(axis)
    if block.size % (count * 8 * 128):
        return lax.psum(block, axis)
    pieces = block.reshape(count, -1, 128)
    vmem = pltpu.VMEM
    summed = pl.pallas_call(
        functools.partial(reduce_kernel, count),
        out_shape=jax.ShapeDtypeStruct(pieces.shape, pieces.dtype),
        in_specs=[pl.BlockSpec(memory_space=vmem)],
        out_specs=pl.BlockSpec(memory_space=vmem),
        scratch_shapes=[
            pltpu.VMEM(pieces.shape, pieces.dtype),
            pltpu.VMEM(pieces.shape, pieces.dtype),
            pltpu.VMEM(pieces.shape[1:], pieces.dtype),
            pltpu.SemaphoreType.DMA((count,)),
            pltpu.SemaphoreType.DMA((count,)),
            pltpu.SemaphoreType.DMA((count,)),
            pltpu.SemaphoreType.DMA((count,)),
        ],
        compiler_params=pltpu.CompilerParams(collective_id=collective, has_side_effects=True),
    )(pieces)
    return summed.reshape(block.shape)


def split_heads(field, count):
    heads = field.shape[1] // HD
    return field.reshape(count, TILE, heads, HD).transpose(2, 0, 1, 3)


def merge_heads(field):
    heads = field.shape[0]
    count = field.shape[1]
    return field.transpose(1, 2, 0, 3).reshape(count * TILE, heads * HD)


def attention_kernel(index_ref, q_ref, do_ref, k_ref, v_ref, att_ref, dq_ref, dk_ref, dv_ref, kbuf, vbuf):
    heads = q_ref.shape[1] // HD
    tiles = q_ref.shape[0] // TILE
    slots = index_ref.shape[0] // (heads * tiles)
    scale = HD ** (-0.5)
    dk_ref[...] = jnp.zeros_like(dk_ref)
    dv_ref[...] = jnp.zeros_like(dv_ref)
    nt = (((1,), (1,)), ((), ()))
    tn = (((0,), (0,)), ((), ()))

    def step(item, carry):
        head = item // tiles
        tile = item % tiles
        cols = pl.ds(pl.multiple_of(head * HD, HD), HD)
        rows = pl.ds(pl.multiple_of(tile * TILE, TILE), TILE)
        picks = [
            pl.ds(pl.multiple_of(index_ref[item * slots + s] * TILE, TILE), TILE)
            for s in range(slots)
        ]
        for s in range(slots):
            kbuf[s * TILE : (s + 1) * TILE, :] = k_ref[picks[s], cols]
            vbuf[s * TILE : (s + 1) * TILE, :] = v_ref[picks[s], cols]
        query = q_ref[rows, cols]
        grad_out = do_ref[rows, cols]
        chosen_keys = kbuf[...]
        chosen_values = vbuf[...]
        scores = (
            lax.dot_general(query, chosen_keys, nt, preferred_element_type=jnp.float32) * scale
        )
        peak = jnp.max(scores, axis=1, keepdims=True)
        log_total = peak + jnp.log(jnp.sum(jnp.exp(scores - peak), axis=1, keepdims=True))
        probs = jnp.exp(scores - log_total)
        weights = probs.astype(jnp.bfloat16)
        attended = jnp.dot(weights, chosen_values, preferred_element_type=jnp.float32).astype(
            jnp.bfloat16
        )
        att_ref[rows, cols] = attended
        delta = jnp.sum(
            grad_out.astype(jnp.float32) * attended.astype(jnp.float32), axis=1, keepdims=True
        )
        grad_probs = lax.dot_general(
            grad_out, chosen_values, nt, preferred_element_type=jnp.float32
        )
        grad_scores = (probs * (grad_probs - delta)).astype(jnp.bfloat16)
        dq_ref[rows, cols] = (
            jnp.dot(grad_scores, chosen_keys, preferred_element_type=jnp.float32) * scale
        ).astype(jnp.bfloat16)
        key_slots = (
            lax.dot_general(grad_scores, query, tn, preferred_element_type=jnp.float32) * scale
        )
        value_slots = lax.dot_general(weights, grad_out, tn, preferred_element_type=jnp.float32)
        for s in range(slots):
            dk_ref[picks[s], cols] += key_slots[s * TILE : (s + 1) * TILE]
            dv_ref[picks[s], cols] += value_slots[s * TILE : (s + 1) * TILE]
        return carry

    lax.fori_loop(0, heads * tiles, step, 0)


def attend(pool_index, query_rows, grad_rows, pool_keys, pool_values):
    count, width = query_rows.shape
    pool_rows = pool_keys.shape[0]
    slots = pool_index.shape[-1]
    vmem = pltpu.VMEM
    flops = 2 * 7 * count * slots * TILE * width
    return pl.pallas_call(
        attention_kernel,
        out_shape=(
            jax.ShapeDtypeStruct((count, width), jnp.bfloat16),
            jax.ShapeDtypeStruct((count, width), jnp.bfloat16),
            jax.ShapeDtypeStruct((pool_rows, width), jnp.float32),
            jax.ShapeDtypeStruct((pool_rows, width), jnp.float32),
        ),
        in_specs=[pl.BlockSpec(memory_space=pltpu.SMEM)] + [pl.BlockSpec(memory_space=vmem)] * 4,
        out_specs=tuple(pl.BlockSpec(memory_space=vmem) for _ in range(4)),
        scratch_shapes=[
            pltpu.VMEM((slots * TILE, HD), jnp.bfloat16),
            pltpu.VMEM((slots * TILE, HD), jnp.bfloat16),
        ],
        compiler_params=pltpu.CompilerParams(vmem_limit_bytes=60 * 1024 * 1024),
        cost_estimate=pl.CostEstimate(
            flops=flops,
            transcendentals=count * slots * TILE * width // HD,
            bytes_accessed=8 * count * width + 12 * pool_rows * width,
        ),
    )(pool_index.reshape(-1), query_rows, grad_rows, pool_keys, pool_values)


def per_device(query, keys, values, cotangent, kv_tiles):
    head_count = lax.axis_size("head")
    cycle_pos = lax.axis_index("blk")
    per_frame = query.shape[0] * head_count // TILE
    reach = -(-HALF // per_frame)
    span = (2 * reach + 1) * per_frame
    global_tiles = kv_tiles[:, 0, :GLOBALS]
    own_tiles = lax.dynamic_slice_in_dim(kv_tiles, cycle_pos * per_frame, per_frame, 1)
    moved_kv = lax.all_to_all(
        jnp.stack([keys, values]), "head", split_axis=2, concat_axis=1, tiled=True
    )
    moved_qg = lax.all_to_all(
        jnp.stack([query, cotangent]), "head", split_axis=2, concat_axis=1, tiled=True
    )
    moved = (moved_qg[0], moved_kv[0], moved_kv[1], moved_qg[1])
    frame_keys = moved[1]
    frame_values = moved[2]
    offset = 1
    earlier = passed_along((frame_keys, frame_values), "blk", offset)
    later = passed_along((frame_keys, frame_values), "blk", -offset)
    earlier_keys = [earlier[0]]
    earlier_values = [earlier[1]]
    later_keys = [later[0]]
    later_values = [later[1]]
    near_keys = jnp.stack(earlier_keys[::-1] + later_keys, axis=0)
    near_values = jnp.stack(earlier_values[::-1] + later_values, axis=0)
    width = frame_keys.shape[1]
    all_keys = jnp.concatenate(
        [near_keys[:reach], frame_keys[None], near_keys[reach:]], axis=0
    ).reshape(span * TILE, width)
    all_values = jnp.concatenate(
        [near_values[:reach], frame_values[None], near_values[reach:]], axis=0
    ).reshape(span * TILE, width)
    heads = width // HD
    tile_ids = cycle_pos * per_frame + jnp.arange(per_frame, dtype=jnp.int32)
    owner = global_tiles[:, :, None] == tile_ids[None, None, :]
    owner_mask = owner.astype(jnp.bfloat16)
    frame_key_tiles = frame_keys.reshape(per_frame, TILE, heads, HD)
    frame_value_tiles = frame_values.reshape(per_frame, TILE, heads, HD)
    global_keys = jnp.einsum(
        "hjt,tkhd->jkhd", owner_mask, frame_key_tiles, preferred_element_type=jnp.float32
    )
    global_values = jnp.einsum(
        "hjt,tkhd->jkhd", owner_mask, frame_value_tiles, preferred_element_type=jnp.float32
    )
    global_both = butterfly_sum(
        jnp.stack([global_keys.astype(jnp.bfloat16), global_values.astype(jnp.bfloat16)]), "blk", 0
    )
    global_rows = GLOBALS * TILE
    pool_keys = jnp.concatenate([all_keys, global_both[0].reshape(global_rows, width)], axis=0)
    pool_values = jnp.concatenate([all_values, global_both[1].reshape(global_rows, width)], axis=0)
    relative = own_tiles - (cycle_pos - reach) * per_frame
    inside = (relative >= 0) & (relative < span)
    matches = own_tiles[:, :, :, None] == global_tiles[:, None, None, :]
    slot_numbers = jnp.arange(global_tiles.shape[1], dtype=jnp.int32)
    global_slot = jnp.sum(jnp.where(matches, slot_numbers[None, None, None, :], 0), axis=-1)
    pool_index = jnp.where(inside, relative, span + global_slot)
    attended, query_rows, key_pool, value_pool = attend(
        pool_index, moved[0], moved[3], pool_keys, pool_values
    )
    frame_rows = per_frame * TILE
    centre = reach * frame_rows
    key_grad = key_pool[centre : centre + frame_rows]
    value_grad = value_pool[centre : centre + frame_rows]
    offset = 1
    lower = (reach - offset) * frame_rows
    returned = passed_along(
        jnp.stack([key_pool[lower : lower + frame_rows], value_pool[lower : lower + frame_rows]]).astype(
            jnp.bfloat16
        ),
        "blk",
        -offset,
    ).astype(jnp.float32)
    key_grad = key_grad + returned[0]
    value_grad = value_grad + returned[1]
    upper = (reach + offset) * frame_rows
    returned = passed_along(
        jnp.stack([key_pool[upper : upper + frame_rows], value_pool[upper : upper + frame_rows]]).astype(
            jnp.bfloat16
        ),
        "blk",
        offset,
    ).astype(jnp.float32)
    key_grad = key_grad + returned[0]
    value_grad = value_grad + returned[1]
    pool_end = span * TILE
    summed = butterfly_sum(
        jnp.stack([key_pool[pool_end:], value_pool[pool_end:]]).reshape(
            2, GLOBALS, TILE, heads, HD
        ),
        "blk",
        1,
    )
    owner_float = owner.astype(jnp.float32)
    key_grad = key_grad + jnp.einsum(
        "hjt,jkhd->tkhd", owner_float, summed[0], precision=lax.Precision.HIGHEST
    ).reshape(frame_rows, width)
    value_grad = value_grad + jnp.einsum(
        "hjt,jkhd->tkhd", owner_float, summed[1], precision=lax.Precision.HIGHEST
    ).reshape(frame_rows, width)
    key_rows = key_grad.astype(jnp.bfloat16)
    value_rows = value_grad.astype(jnp.bfloat16)
    forward_back = lax.all_to_all(
        jnp.stack([attended, query_rows]), "head", split_axis=1, concat_axis=2, tiled=True
    )
    backward_back = lax.all_to_all(
        jnp.stack([key_rows, value_rows]), "head", split_axis=1, concat_axis=2, tiled=True
    )
    results = (forward_back[0], forward_back[1], backward_back[0], backward_back[1])
    return (results[0], results[1], results[2], results[3])


def solution(mesh):
    placed = (
        P(("blk", "head"), None),
        P(("blk", "head"), None),
        P(("blk", "head"), None),
        P(("blk", "head"), None),
        P("head", None, None),
    )
    return jax.shard_map(
        per_device,
        mesh=mesh,
        in_specs=placed,
        out_specs=(
            P(("blk", "head"), None),
            P(("blk", "head"), None),
            P(("blk", "head"), None),
            P(("blk", "head"), None),
        ),
        check_vma=False,
    )
```

```python
import functools

import jax
import jax.numpy as jnp
from jax import lax
from jax.experimental import pallas as pl
from jax.experimental.pallas import tpu as pltpu
from jax.sharding import PartitionSpec as P

MESH = pl.DeviceIdType.MESH
HD = 128
TILE = 128
GLOBALS = 2
HALF = 8


def passed_along(block, axis, distance):
    devices = range(lax.axis_size(axis))
    route = [(i - distance, i) for i in devices if i - distance in devices]
    return lax.ppermute(block, axis, route)


def reduce_kernel(count, x_ref, out_ref, inbox, gathered, mine, send_sem, recv_sem, back_send, back_recv):
    me = lax.axis_index("blk")
    column = lax.axis_index("head")
    barrier = pltpu.get_barrier_semaphore()
    for k in range(1, count):
        pl.semaphore_signal(
            barrier, 1, device_id=(lax.rem(me + k, count), column), device_id_type=MESH
        )
    pl.semaphore_wait(barrier, count - 1)
    outgoing = []
    for k in range(1, count):
        peer = lax.rem(me + k, count)
        copy = pltpu.make_async_remote_copy(
            src_ref=x_ref.at[peer],
            dst_ref=inbox.at[me],
            send_sem=send_sem.at[k],
            recv_sem=recv_sem.at[me],
            device_id=(peer, column),
            device_id_type=MESH,
        )
        copy.start()
        outgoing.append(copy)
    total = x_ref[me].astype(jnp.float32)
    for k in range(1, count):
        source = lax.rem(me + count - k, count)
        pltpu.make_async_remote_copy(
            src_ref=x_ref.at[source],
            dst_ref=inbox.at[source],
            send_sem=send_sem.at[k],
            recv_sem=recv_sem.at[source],
            device_id=(source, column),
            device_id_type=MESH,
        ).wait_recv()
        total = total + inbox[source].astype(jnp.float32)
    mine[...] = total.astype(mine.dtype)
    for k in range(1, count):
        peer = lax.rem(me + k, count)
        copy = pltpu.make_async_remote_copy(
            src_ref=mine,
            dst_ref=gathered.at[me],
            send_sem=back_send.at[k],
            recv_sem=back_recv.at[me],
            device_id=(peer, column),
            device_id_type=MESH,
        )
        copy.start()
        outgoing.append(copy)
    gathered[me] = mine[...]
    for k in range(1, count):
        source = lax.rem(me + count - k, count)
        pltpu.make_async_remote_copy(
            src_ref=mine,
            dst_ref=gathered.at[source],
            send_sem=back_send.at[k],
            recv_sem=back_recv.at[source],
            device_id=(source, column),
            device_id_type=MESH,
        ).wait_recv()
    for copy in outgoing:
        copy.wait_send()
    out_ref[...] = gathered[...]


def butterfly_sum(block, axis, collective):
    count = lax.axis_size(axis)
    if block.size % (count * 8 * 128):
        return lax.psum(block, axis)
    pieces = block.reshape(count, -1, 128)
    vmem = pltpu.VMEM
    summed = pl.pallas_call(
        functools.partial(reduce_kernel, count),
        out_shape=jax.ShapeDtypeStruct(pieces.shape, pieces.dtype),
        in_specs=[pl.BlockSpec(memory_space=vmem)],
        out_specs=pl.BlockSpec(memory_space=vmem),
        scratch_shapes=[
            pltpu.VMEM(pieces.shape, pieces.dtype),
            pltpu.VMEM(pieces.shape, pieces.dtype),
            pltpu.VMEM(pieces.shape[1:], pieces.dtype),
            pltpu.SemaphoreType.DMA((count,)),
            pltpu.SemaphoreType.DMA((count,)),
            pltpu.SemaphoreType.DMA((count,)),
            pltpu.SemaphoreType.DMA((count,)),
        ],
        compiler_params=pltpu.CompilerParams(collective_id=collective, has_side_effects=True),
    )(pieces)
    return summed.reshape(block.shape)


def split_heads(field, count):
    heads = field.shape[1] // HD
    return field.reshape(count, TILE, heads, HD).transpose(2, 0, 1, 3)


def merge_heads(field):
    heads = field.shape[0]
    count = field.shape[1]
    return field.transpose(1, 2, 0, 3).reshape(count * TILE, heads * HD)


def attention_kernel(
    edges, index_ref, q_ref, do_ref, k_ref, v_ref, att_ref, dq_ref, dk_ref, dv_ref, near_ref, kbuf, vbuf
):
    heads = q_ref.shape[1] // HD
    tiles = q_ref.shape[0] // TILE
    slots = index_ref.shape[0] // (heads * tiles)
    scale = HD ** (-0.5)
    dk_ref[...] = jnp.zeros_like(dk_ref)
    dv_ref[...] = jnp.zeros_like(dv_ref)
    nt = (((1,), (1,)), ((), ()))
    tn = (((0,), (0,)), ((), ()))

    def step(item, carry):
        head = item // tiles
        tile = item % tiles
        cols = pl.ds(pl.multiple_of(head * HD, HD), HD)
        rows = pl.ds(pl.multiple_of(tile * TILE, TILE), TILE)
        picks = [
            pl.ds(pl.multiple_of(index_ref[item * slots + s] * TILE, TILE), TILE)
            for s in range(slots)
        ]
        for s in range(slots):
            kbuf[s * TILE : (s + 1) * TILE, :] = k_ref[picks[s], cols]
            vbuf[s * TILE : (s + 1) * TILE, :] = v_ref[picks[s], cols]
        query = q_ref[rows, cols]
        grad_out = do_ref[rows, cols]
        chosen_keys = kbuf[...]
        chosen_values = vbuf[...]
        scores = (
            lax.dot_general(query, chosen_keys, nt, preferred_element_type=jnp.float32) * scale
        )
        peak = jnp.max(scores, axis=1, keepdims=True)
        log_total = peak + jnp.log(jnp.sum(jnp.exp(scores - peak), axis=1, keepdims=True))
        probs = jnp.exp(scores - log_total)
        weights = probs.astype(jnp.bfloat16)
        attended = jnp.dot(weights, chosen_values, preferred_element_type=jnp.float32).astype(
            jnp.bfloat16
        )
        att_ref[rows, cols] = attended
        delta = jnp.sum(
            grad_out.astype(jnp.float32) * attended.astype(jnp.float32), axis=1, keepdims=True
        )
        grad_probs = lax.dot_general(
            grad_out, chosen_values, nt, preferred_element_type=jnp.float32
        )
        grad_scores = (probs * (grad_probs - delta)).astype(jnp.bfloat16)
        dq_ref[rows, cols] = (
            jnp.dot(grad_scores, chosen_keys, preferred_element_type=jnp.float32) * scale
        ).astype(jnp.bfloat16)
        key_slots = (
            lax.dot_general(grad_scores, query, tn, preferred_element_type=jnp.float32) * scale
        )
        value_slots = lax.dot_general(weights, grad_out, tn, preferred_element_type=jnp.float32)
        for s in range(slots):
            dk_ref[picks[s], cols] += key_slots[s * TILE : (s + 1) * TILE]
            dv_ref[picks[s], cols] += value_slots[s * TILE : (s + 1) * TILE]
        return carry

    lax.fori_loop(0, heads * tiles, step, 0)
    span_rows = near_ref.shape[1]
    for part, start in enumerate(edges):
        for row in range(0, span_rows, TILE):
            near_ref[2 * part, row : row + TILE, :] = dk_ref[
                start + row : start + row + TILE, :
            ].astype(jnp.bfloat16)
            near_ref[2 * part + 1, row : row + TILE, :] = dv_ref[
                start + row : start + row + TILE, :
            ].astype(jnp.bfloat16)


def attend(pool_index, query_rows, grad_rows, pool_keys, pool_values, edges):
    count, width = query_rows.shape
    pool_rows = pool_keys.shape[0]
    slots = pool_index.shape[-1]
    vmem = pltpu.VMEM
    flops = 2 * 7 * count * slots * TILE * width
    return pl.pallas_call(
        functools.partial(attention_kernel, edges),
        out_shape=(
            jax.ShapeDtypeStruct((count, width), jnp.bfloat16),
            jax.ShapeDtypeStruct((count, width), jnp.bfloat16),
            jax.ShapeDtypeStruct((pool_rows, width), jnp.float32),
            jax.ShapeDtypeStruct((pool_rows, width), jnp.float32),
            jax.ShapeDtypeStruct((2 * len(edges), count, width), jnp.bfloat16),
        ),
        in_specs=[pl.BlockSpec(memory_space=pltpu.SMEM)] + [pl.BlockSpec(memory_space=vmem)] * 4,
        out_specs=tuple(pl.BlockSpec(memory_space=vmem) for _ in range(5)),
        scratch_shapes=[
            pltpu.VMEM((slots * TILE, HD), jnp.bfloat16),
            pltpu.VMEM((slots * TILE, HD), jnp.bfloat16),
        ],
        compiler_params=pltpu.CompilerParams(vmem_limit_bytes=60 * 1024 * 1024),
        cost_estimate=pl.CostEstimate(
            flops=flops,
            transcendentals=count * slots * TILE * width // HD,
            bytes_accessed=8 * count * width + 12 * pool_rows * width,
        ),
    )(pool_index.reshape(-1), query_rows, grad_rows, pool_keys, pool_values)


def per_device(query, keys, values, cotangent, kv_tiles):
    head_count = lax.axis_size("head")
    cycle_pos = lax.axis_index("blk")
    per_frame = query.shape[0] * head_count // TILE
    reach = -(-HALF // per_frame)
    span = (2 * reach + 1) * per_frame
    global_tiles = kv_tiles[:, 0, :GLOBALS]
    own_tiles = lax.dynamic_slice_in_dim(kv_tiles, cycle_pos * per_frame, per_frame, 1)
    moved_kv = lax.all_to_all(
        jnp.stack([keys, values]), "head", split_axis=2, concat_axis=1, tiled=True
    )
    moved_qg = lax.all_to_all(
        jnp.stack([query, cotangent]), "head", split_axis=2, concat_axis=1, tiled=True
    )
    moved = (moved_qg[0], moved_kv[0], moved_kv[1], moved_qg[1])
    frame_keys = moved[1]
    frame_values = moved[2]
    offset = 1
    earlier = passed_along((frame_keys, frame_values), "blk", offset)
    later = passed_along((frame_keys, frame_values), "blk", -offset)
    earlier_keys = [earlier[0]]
    earlier_values = [earlier[1]]
    later_keys = [later[0]]
    later_values = [later[1]]
    near_keys = jnp.stack(earlier_keys[::-1] + later_keys, axis=0)
    near_values = jnp.stack(earlier_values[::-1] + later_values, axis=0)
    width = frame_keys.shape[1]
    all_keys = jnp.concatenate(
        [near_keys[:reach], frame_keys[None], near_keys[reach:]], axis=0
    ).reshape(span * TILE, width)
    all_values = jnp.concatenate(
        [near_values[:reach], frame_values[None], near_values[reach:]], axis=0
    ).reshape(span * TILE, width)
    heads = width // HD
    tile_ids = cycle_pos * per_frame + jnp.arange(per_frame, dtype=jnp.int32)
    owner = global_tiles[:, :, None] == tile_ids[None, None, :]
    owner_mask = owner.astype(jnp.bfloat16)
    frame_key_tiles = frame_keys.reshape(per_frame, TILE, heads, HD)
    frame_value_tiles = frame_values.reshape(per_frame, TILE, heads, HD)
    global_keys = jnp.einsum(
        "hjt,tkhd->jkhd", owner_mask, frame_key_tiles, preferred_element_type=jnp.float32
    )
    global_values = jnp.einsum(
        "hjt,tkhd->jkhd", owner_mask, frame_value_tiles, preferred_element_type=jnp.float32
    )
    global_both = butterfly_sum(
        jnp.stack([global_keys.astype(jnp.bfloat16), global_values.astype(jnp.bfloat16)]), "blk", 0
    )
    global_rows = GLOBALS * TILE
    pool_keys = jnp.concatenate([all_keys, global_both[0].reshape(global_rows, width)], axis=0)
    pool_values = jnp.concatenate([all_values, global_both[1].reshape(global_rows, width)], axis=0)
    relative = own_tiles - (cycle_pos - reach) * per_frame
    inside = (relative >= 0) & (relative < span)
    matches = own_tiles[:, :, :, None] == global_tiles[:, None, None, :]
    slot_numbers = jnp.arange(global_tiles.shape[1], dtype=jnp.int32)
    global_slot = jnp.sum(jnp.where(matches, slot_numbers[None, None, None, :], 0), axis=-1)
    pool_index = jnp.where(inside, relative, span + global_slot)
    frame_rows = per_frame * TILE
    edges = ((reach - 1) * frame_rows, (reach + 1) * frame_rows)
    attended, query_rows, key_pool, value_pool, near = attend(
        pool_index, moved[0], moved[3], pool_keys, pool_values, edges
    )
    centre = reach * frame_rows
    key_grad = key_pool[centre : centre + frame_rows]
    value_grad = value_pool[centre : centre + frame_rows]
    offset = 1
    lower = (reach - offset) * frame_rows
    returned = (
        passed_along(
            near[0], "blk", -offset
        ).astype(jnp.float32),
        passed_along(
            near[1], "blk", -offset
        ).astype(jnp.float32),
    )
    key_grad = key_grad + returned[0]
    value_grad = value_grad + returned[1]
    upper = (reach + offset) * frame_rows
    returned = (
        passed_along(
            near[2], "blk", offset
        ).astype(jnp.float32),
        passed_along(
            near[3], "blk", offset
        ).astype(jnp.float32),
    )
    key_grad = key_grad + returned[0]
    value_grad = value_grad + returned[1]
    pool_end = span * TILE
    summed = butterfly_sum(
        jnp.stack([key_pool[pool_end:], value_pool[pool_end:]]).reshape(
            2, GLOBALS, TILE, heads, HD
        ),
        "blk",
        1,
    )
    owner_float = owner.astype(jnp.float32)
    key_grad = key_grad + jnp.einsum(
        "hjt,jkhd->tkhd", owner_float, summed[0], precision=lax.Precision.HIGHEST
    ).reshape(frame_rows, width)
    value_grad = value_grad + jnp.einsum(
        "hjt,jkhd->tkhd", owner_float, summed[1], precision=lax.Precision.HIGHEST
    ).reshape(frame_rows, width)
    key_rows = key_grad.astype(jnp.bfloat16)
    value_rows = value_grad.astype(jnp.bfloat16)
    forward_back = lax.all_to_all(
        jnp.stack([attended, query_rows]), "head", split_axis=1, concat_axis=2, tiled=True
    )
    backward_back = lax.all_to_all(
        jnp.stack([key_rows, value_rows]), "head", split_axis=1, concat_axis=2, tiled=True
    )
    results = (forward_back[0], forward_back[1], backward_back[0], backward_back[1])
    return (results[0], results[1], results[2], results[3])


def solution(mesh):
    placed = (
        P(("blk", "head"), None),
        P(("blk", "head"), None),
        P(("blk", "head"), None),
        P(("blk", "head"), None),
        P("head", None, None),
    )
    return jax.shard_map(
        per_device,
        mesh=mesh,
        in_specs=placed,
        out_specs=(
            P(("blk", "head"), None),
            P(("blk", "head"), None),
            P(("blk", "head"), None),
            P(("blk", "head"), None),
        ),
        check_vma=False,
    )
```

```python
import functools

import jax
import jax.numpy as jnp
from jax import lax
from jax.experimental import pallas as pl
from jax.experimental.pallas import tpu as pltpu
from jax.sharding import PartitionSpec as P

MESH = pl.DeviceIdType.MESH
HD = 128
TILE = 128
GLOBALS = 2
HALF = 8


def passed_along(block, axis, distance):
    devices = range(lax.axis_size(axis))
    route = [(i - distance, i) for i in devices if i - distance in devices]
    return lax.ppermute(block, axis, route)


def reduce_kernel(count, x_ref, out_ref, inbox, gathered, mine, send_sem, recv_sem, back_send, back_recv):
    me = lax.axis_index("blk")
    column = lax.axis_index("head")
    barrier = pltpu.get_barrier_semaphore()
    for k in range(1, count):
        pl.semaphore_signal(
            barrier, 1, device_id=(lax.rem(me + k, count), column), device_id_type=MESH
        )
    pl.semaphore_wait(barrier, count - 1)
    outgoing = []
    for k in range(1, count):
        peer = lax.rem(me + k, count)
        copy = pltpu.make_async_remote_copy(
            src_ref=x_ref.at[peer],
            dst_ref=inbox.at[me],
            send_sem=send_sem.at[k],
            recv_sem=recv_sem.at[me],
            device_id=(peer, column),
            device_id_type=MESH,
        )
        copy.start()
        outgoing.append(copy)
    total = x_ref[me].astype(jnp.float32)
    for k in range(1, count):
        source = lax.rem(me + count - k, count)
        pltpu.make_async_remote_copy(
            src_ref=x_ref.at[source],
            dst_ref=inbox.at[source],
            send_sem=send_sem.at[k],
            recv_sem=recv_sem.at[source],
            device_id=(source, column),
            device_id_type=MESH,
        ).wait_recv()
        total = total + inbox[source].astype(jnp.float32)
    mine[...] = total.astype(mine.dtype)
    for k in range(1, count):
        peer = lax.rem(me + k, count)
        copy = pltpu.make_async_remote_copy(
            src_ref=mine,
            dst_ref=gathered.at[me],
            send_sem=back_send.at[k],
            recv_sem=back_recv.at[me],
            device_id=(peer, column),
            device_id_type=MESH,
        )
        copy.start()
        outgoing.append(copy)
    gathered[me] = mine[...]
    for k in range(1, count):
        source = lax.rem(me + count - k, count)
        pltpu.make_async_remote_copy(
            src_ref=mine,
            dst_ref=gathered.at[source],
            send_sem=back_send.at[k],
            recv_sem=back_recv.at[source],
            device_id=(source, column),
            device_id_type=MESH,
        ).wait_recv()
    for copy in outgoing:
        copy.wait_send()
    out_ref[...] = gathered[...]


def butterfly_sum(block, axis, collective):
    count = lax.axis_size(axis)
    if block.size % (count * 8 * 128):
        return lax.psum(block, axis)
    pieces = block.reshape(count, -1, 128)
    vmem = pltpu.VMEM
    summed = pl.pallas_call(
        functools.partial(reduce_kernel, count),
        out_shape=jax.ShapeDtypeStruct(pieces.shape, pieces.dtype),
        in_specs=[pl.BlockSpec(memory_space=vmem)],
        out_specs=pl.BlockSpec(memory_space=vmem),
        scratch_shapes=[
            pltpu.VMEM(pieces.shape, pieces.dtype),
            pltpu.VMEM(pieces.shape, pieces.dtype),
            pltpu.VMEM(pieces.shape[1:], pieces.dtype),
            pltpu.SemaphoreType.DMA((count,)),
            pltpu.SemaphoreType.DMA((count,)),
            pltpu.SemaphoreType.DMA((count,)),
            pltpu.SemaphoreType.DMA((count,)),
        ],
        compiler_params=pltpu.CompilerParams(collective_id=collective, has_side_effects=True),
    )(pieces)
    return summed.reshape(block.shape)


def split_heads(field, count):
    heads = field.shape[1] // HD
    return field.reshape(count, TILE, heads, HD).transpose(2, 0, 1, 3)


def merge_heads(field):
    heads = field.shape[0]
    count = field.shape[1]
    return field.transpose(1, 2, 0, 3).reshape(count * TILE, heads * HD)


def attention_kernel(index_ref, q_ref, do_ref, k_ref, v_ref, att_ref, dq_ref, dk_ref, dv_ref, kbuf, vbuf):
    heads = q_ref.shape[1] // HD
    tiles = q_ref.shape[0] // TILE
    slots = index_ref.shape[0] // (heads * tiles)
    scale = HD ** (-0.5)
    dk_ref[...] = jnp.zeros_like(dk_ref)
    dv_ref[...] = jnp.zeros_like(dv_ref)
    nt = (((1,), (1,)), ((), ()))
    tn = (((0,), (0,)), ((), ()))

    def step(item, carry):
        head = item // tiles
        tile = item % tiles
        cols = pl.ds(pl.multiple_of(head * HD, HD), HD)
        rows = pl.ds(pl.multiple_of(tile * TILE, TILE), TILE)
        picks = [
            pl.ds(pl.multiple_of(index_ref[item * slots + s] * TILE, TILE), TILE)
            for s in range(slots)
        ]
        for s in range(slots):
            kbuf[s * TILE : (s + 1) * TILE, :] = k_ref[picks[s], cols]
            vbuf[s * TILE : (s + 1) * TILE, :] = v_ref[picks[s], cols]
        query = q_ref[rows, cols]
        grad_out = do_ref[rows, cols]
        chosen_keys = kbuf[...]
        chosen_values = vbuf[...]
        scores = (
            lax.dot_general(query, chosen_keys, nt, preferred_element_type=jnp.float32) * scale
        )
        peak = jnp.max(scores, axis=1, keepdims=True)
        log_total = peak + jnp.log(jnp.sum(jnp.exp(scores - peak), axis=1, keepdims=True))
        probs = jnp.exp(scores - log_total)
        weights = probs.astype(jnp.bfloat16)
        attended = jnp.dot(weights, chosen_values, preferred_element_type=jnp.float32).astype(
            jnp.bfloat16
        )
        att_ref[rows, cols] = attended
        delta = jnp.sum(
            grad_out.astype(jnp.float32) * attended.astype(jnp.float32), axis=1, keepdims=True
        )
        grad_probs = lax.dot_general(
            grad_out, chosen_values, nt, preferred_element_type=jnp.float32
        )
        grad_scores = (probs * (grad_probs - delta)).astype(jnp.bfloat16)
        dq_ref[rows, cols] = (
            jnp.dot(grad_scores, chosen_keys, preferred_element_type=jnp.float32) * scale
        ).astype(jnp.bfloat16)
        key_slots = (
            lax.dot_general(grad_scores, query, tn, preferred_element_type=jnp.float32) * scale
        )
        value_slots = lax.dot_general(weights, grad_out, tn, preferred_element_type=jnp.float32)
        for s in range(slots):
            dk_ref[picks[s], cols] += key_slots[s * TILE : (s + 1) * TILE]
            dv_ref[picks[s], cols] += value_slots[s * TILE : (s + 1) * TILE]
        return carry

    lax.fori_loop(0, heads * tiles, step, 0)


def attend(pool_index, query_rows, grad_rows, pool_keys, pool_values):
    count, width = query_rows.shape
    pool_rows = pool_keys.shape[0]
    slots = pool_index.shape[-1]
    vmem = pltpu.VMEM
    flops = 2 * 7 * count * slots * TILE * width
    return pl.pallas_call(
        attention_kernel,
        out_shape=(
            jax.ShapeDtypeStruct((count, width), jnp.bfloat16),
            jax.ShapeDtypeStruct((count, width), jnp.bfloat16),
            jax.ShapeDtypeStruct((pool_rows, width), jnp.float32),
            jax.ShapeDtypeStruct((pool_rows, width), jnp.float32),
        ),
        in_specs=[pl.BlockSpec(memory_space=pltpu.SMEM)] + [pl.BlockSpec(memory_space=vmem)] * 4,
        out_specs=tuple(pl.BlockSpec(memory_space=vmem) for _ in range(4)),
        scratch_shapes=[
            pltpu.VMEM((slots * TILE, HD), jnp.bfloat16),
            pltpu.VMEM((slots * TILE, HD), jnp.bfloat16),
        ],
        compiler_params=pltpu.CompilerParams(vmem_limit_bytes=60 * 1024 * 1024),
        cost_estimate=pl.CostEstimate(
            flops=flops,
            transcendentals=count * slots * TILE * width // HD,
            bytes_accessed=8 * count * width + 12 * pool_rows * width,
        ),
    )(pool_index.reshape(-1), query_rows, grad_rows, pool_keys, pool_values)


def per_device(query, keys, values, cotangent, kv_tiles):
    head_count = lax.axis_size("head")
    cycle_pos = lax.axis_index("blk")
    per_frame = query.shape[0] * head_count // TILE
    reach = -(-HALF // per_frame)
    span = (2 * reach + 1) * per_frame
    global_tiles = kv_tiles[:, 0, :GLOBALS]
    own_tiles = lax.dynamic_slice_in_dim(kv_tiles, cycle_pos * per_frame, per_frame, 1)
    moved_kv = lax.all_to_all(
        jnp.stack([keys, values]), "head", split_axis=2, concat_axis=1, tiled=True
    )
    moved_qg = lax.all_to_all(
        jnp.stack([query, cotangent]), "head", split_axis=2, concat_axis=1, tiled=True
    )
    moved = (moved_qg[0], moved_kv[0], moved_kv[1], moved_qg[1])
    frame_keys = moved[1]
    frame_values = moved[2]
    offset = 1
    earlier = passed_along((frame_keys, frame_values), "blk", offset)
    later = passed_along((frame_keys, frame_values), "blk", -offset)
    earlier_keys = [earlier[0]]
    earlier_values = [earlier[1]]
    later_keys = [later[0]]
    later_values = [later[1]]
    near_keys = jnp.stack(earlier_keys[::-1] + later_keys, axis=0)
    near_values = jnp.stack(earlier_values[::-1] + later_values, axis=0)
    width = frame_keys.shape[1]
    all_keys = jnp.concatenate(
        [near_keys[:reach], frame_keys[None], near_keys[reach:]], axis=0
    ).reshape(span * TILE, width)
    all_values = jnp.concatenate(
        [near_values[:reach], frame_values[None], near_values[reach:]], axis=0
    ).reshape(span * TILE, width)
    heads = width // HD
    tile_ids = cycle_pos * per_frame + jnp.arange(per_frame, dtype=jnp.int32)
    owner = global_tiles[:, :, None] == tile_ids[None, None, :]
    owner_mask = owner.astype(jnp.bfloat16)
    frame_key_tiles = frame_keys.reshape(per_frame, TILE, heads, HD)
    frame_value_tiles = frame_values.reshape(per_frame, TILE, heads, HD)
    global_keys = jnp.einsum(
        "hjt,tkhd->jkhd", owner_mask, frame_key_tiles, preferred_element_type=jnp.float32
    )
    global_values = jnp.einsum(
        "hjt,tkhd->jkhd", owner_mask, frame_value_tiles, preferred_element_type=jnp.float32
    )
    global_both = butterfly_sum(
        jnp.stack([global_keys.astype(jnp.bfloat16), global_values.astype(jnp.bfloat16)]), "blk", 0
    )
    global_rows = GLOBALS * TILE
    pool_keys = jnp.concatenate([all_keys, global_both[0].reshape(global_rows, width)], axis=0)
    pool_values = jnp.concatenate([all_values, global_both[1].reshape(global_rows, width)], axis=0)
    relative = own_tiles - (cycle_pos - reach) * per_frame
    inside = (relative >= 0) & (relative < span)
    matches = own_tiles[:, :, :, None] == global_tiles[:, None, None, :]
    slot_numbers = jnp.arange(global_tiles.shape[1], dtype=jnp.int32)
    global_slot = jnp.sum(jnp.where(matches, slot_numbers[None, None, None, :], 0), axis=-1)
    pool_index = jnp.where(inside, relative, span + global_slot)
    attended, query_rows, key_pool, value_pool = attend(
        pool_index, moved[0], moved[3], pool_keys, pool_values
    )
    frame_rows = per_frame * TILE
    centre = reach * frame_rows
    key_grad = key_pool[centre : centre + frame_rows]
    value_grad = value_pool[centre : centre + frame_rows]
    offset = 1
    lower = (reach - offset) * frame_rows
    returned = (
        passed_along(
            key_pool[lower : lower + frame_rows].astype(jnp.bfloat16), "blk", -offset
        ).astype(jnp.float32),
        passed_along(
            value_pool[lower : lower + frame_rows].astype(jnp.bfloat16), "blk", -offset
        ).astype(jnp.float32),
    )
    key_grad = key_grad + returned[0]
    value_grad = value_grad + returned[1]
    upper = (reach + offset) * frame_rows
    returned = (
        passed_along(
            key_pool[upper : upper + frame_rows].astype(jnp.bfloat16), "blk", offset
        ).astype(jnp.float32),
        passed_along(
            value_pool[upper : upper + frame_rows].astype(jnp.bfloat16), "blk", offset
        ).astype(jnp.float32),
    )
    key_grad = key_grad + returned[0]
    value_grad = value_grad + returned[1]
    pool_end = span * TILE
    summed = butterfly_sum(
        jnp.stack([key_pool[pool_end:], value_pool[pool_end:]]).reshape(
            2, GLOBALS, TILE, heads, HD
        ),
        "blk",
        1,
    )
    owner_float = owner.astype(jnp.float32)
    key_grad = key_grad + jnp.einsum(
        "hjt,jkhd->tkhd", owner_float, summed[0], precision=lax.Precision.HIGHEST
    ).reshape(frame_rows, width)
    value_grad = value_grad + jnp.einsum(
        "hjt,jkhd->tkhd", owner_float, summed[1], precision=lax.Precision.HIGHEST
    ).reshape(frame_rows, width)
    key_rows = key_grad.astype(jnp.bfloat16)
    value_rows = value_grad.astype(jnp.bfloat16)
    forward_back = lax.all_to_all(
        jnp.stack([attended, query_rows]), "head", split_axis=1, concat_axis=2, tiled=True
    )
    key_back = lax.all_to_all(key_rows, "head", split_axis=0, concat_axis=1, tiled=True)
    value_back = lax.all_to_all(value_rows, "head", split_axis=0, concat_axis=1, tiled=True)
    results = (forward_back[0], forward_back[1], key_back, value_back)
    return (results[0], results[1], results[2], results[3])


def solution(mesh):
    placed = (
        P(("blk", "head"), None),
        P(("blk", "head"), None),
        P(("blk", "head"), None),
        P(("blk", "head"), None),
        P("head", None, None),
    )
    return jax.shard_map(
        per_device,
        mesh=mesh,
        in_specs=placed,
        out_specs=(
            P(("blk", "head"), None),
            P(("blk", "head"), None),
            P(("blk", "head"), None),
            P(("blk", "head"), None),
        ),
        check_vma=False,
    )
```

```python
import functools

import jax
import jax.numpy as jnp
from jax import lax
from jax.experimental import pallas as pl
from jax.experimental.pallas import tpu as pltpu
from jax.sharding import PartitionSpec as P

MESH = pl.DeviceIdType.MESH
HD = 128
TILE = 128
GLOBALS = 2
HALF = 8


def passed_along(block, axis, distance):
    devices = range(lax.axis_size(axis))
    route = [(i - distance, i) for i in devices if i - distance in devices]
    return lax.ppermute(block, axis, route)


def reduce_kernel(count, x_ref, out_ref, inbox, gathered, mine, send_sem, recv_sem, back_send, back_recv):
    me = lax.axis_index("blk")
    column = lax.axis_index("head")
    barrier = pltpu.get_barrier_semaphore()
    for k in range(1, count):
        pl.semaphore_signal(
            barrier, 1, device_id=(lax.rem(me + k, count), column), device_id_type=MESH
        )
    pl.semaphore_wait(barrier, count - 1)
    outgoing = []
    for k in range(1, count):
        peer = lax.rem(me + k, count)
        copy = pltpu.make_async_remote_copy(
            src_ref=x_ref.at[peer],
            dst_ref=inbox.at[me],
            send_sem=send_sem.at[k],
            recv_sem=recv_sem.at[me],
            device_id=(peer, column),
            device_id_type=MESH,
        )
        copy.start()
        outgoing.append(copy)
    total = x_ref[me].astype(jnp.float32)
    for k in range(1, count):
        source = lax.rem(me + count - k, count)
        pltpu.make_async_remote_copy(
            src_ref=x_ref.at[source],
            dst_ref=inbox.at[source],
            send_sem=send_sem.at[k],
            recv_sem=recv_sem.at[source],
            device_id=(source, column),
            device_id_type=MESH,
        ).wait_recv()
        total = total + inbox[source].astype(jnp.float32)
    mine[...] = total.astype(mine.dtype)
    for k in range(1, count):
        peer = lax.rem(me + k, count)
        copy = pltpu.make_async_remote_copy(
            src_ref=mine,
            dst_ref=gathered.at[me],
            send_sem=back_send.at[k],
            recv_sem=back_recv.at[me],
            device_id=(peer, column),
            device_id_type=MESH,
        )
        copy.start()
        outgoing.append(copy)
    gathered[me] = mine[...]
    for k in range(1, count):
        source = lax.rem(me + count - k, count)
        pltpu.make_async_remote_copy(
            src_ref=mine,
            dst_ref=gathered.at[source],
            send_sem=back_send.at[k],
            recv_sem=back_recv.at[source],
            device_id=(source, column),
            device_id_type=MESH,
        ).wait_recv()
    for copy in outgoing:
        copy.wait_send()
    out_ref[...] = gathered[...]


def butterfly_sum(block, axis, collective):
    count = lax.axis_size(axis)
    if block.size % (count * 8 * 128):
        return lax.psum(block, axis)
    pieces = block.reshape(count, -1, 128)
    vmem = pltpu.VMEM
    summed = pl.pallas_call(
        functools.partial(reduce_kernel, count),
        out_shape=jax.ShapeDtypeStruct(pieces.shape, pieces.dtype),
        in_specs=[pl.BlockSpec(memory_space=vmem)],
        out_specs=pl.BlockSpec(memory_space=vmem),
        scratch_shapes=[
            pltpu.VMEM(pieces.shape, pieces.dtype),
            pltpu.VMEM(pieces.shape, pieces.dtype),
            pltpu.VMEM(pieces.shape[1:], pieces.dtype),
            pltpu.SemaphoreType.DMA((count,)),
            pltpu.SemaphoreType.DMA((count,)),
            pltpu.SemaphoreType.DMA((count,)),
            pltpu.SemaphoreType.DMA((count,)),
        ],
        compiler_params=pltpu.CompilerParams(collective_id=collective, has_side_effects=True),
    )(pieces)
    return summed.reshape(block.shape)


def split_heads(field, count):
    heads = field.shape[1] // HD
    return field.reshape(count, TILE, heads, HD).transpose(2, 0, 1, 3)


def merge_heads(field):
    heads = field.shape[0]
    count = field.shape[1]
    return field.transpose(1, 2, 0, 3).reshape(count * TILE, heads * HD)


def attention_kernel(index_ref, q_ref, do_ref, k_ref, v_ref, att_ref, dq_ref, dk_ref, dv_ref, kbuf, vbuf):
    heads = q_ref.shape[1] // HD
    tiles = q_ref.shape[0] // TILE
    slots = index_ref.shape[0] // (heads * tiles)
    scale = HD ** (-0.5)
    dk_ref[...] = jnp.zeros_like(dk_ref)
    dv_ref[...] = jnp.zeros_like(dv_ref)
    nt = (((1,), (1,)), ((), ()))
    tn = (((0,), (0,)), ((), ()))

    def step(item, carry):
        head = item // tiles
        tile = item % tiles
        cols = pl.ds(pl.multiple_of(head * HD, HD), HD)
        rows = pl.ds(pl.multiple_of(tile * TILE, TILE), TILE)
        picks = [
            pl.ds(pl.multiple_of(index_ref[item * slots + s] * TILE, TILE), TILE)
            for s in range(slots)
        ]
        for s in range(slots):
            kbuf[s * TILE : (s + 1) * TILE, :] = k_ref[picks[s], cols]
            vbuf[s * TILE : (s + 1) * TILE, :] = v_ref[picks[s], cols]
        query = q_ref[rows, cols]
        grad_out = do_ref[rows, cols]
        chosen_keys = kbuf[...]
        chosen_values = vbuf[...]
        scores = (
            lax.dot_general(query, chosen_keys, nt, preferred_element_type=jnp.float32) * scale
        )
        peak = jnp.max(scores, axis=1, keepdims=True)
        log_total = peak + jnp.log(jnp.sum(jnp.exp(scores - peak), axis=1, keepdims=True))
        probs = jnp.exp(scores - log_total)
        weights = probs.astype(jnp.bfloat16)
        attended = jnp.dot(weights, chosen_values, preferred_element_type=jnp.float32).astype(
            jnp.bfloat16
        )
        att_ref[rows, cols] = attended
        delta = jnp.sum(
            grad_out.astype(jnp.float32) * attended.astype(jnp.float32), axis=1, keepdims=True
        )
        grad_probs = lax.dot_general(
            grad_out, chosen_values, nt, preferred_element_type=jnp.float32
        )
        grad_scores = (probs * (grad_probs - delta)).astype(jnp.bfloat16)
        dq_ref[rows, cols] = (
            jnp.dot(grad_scores, chosen_keys, preferred_element_type=jnp.float32) * scale
        ).astype(jnp.bfloat16)
        key_slots = (
            lax.dot_general(grad_scores, query, tn, preferred_element_type=jnp.float32) * scale
        )
        value_slots = lax.dot_general(weights, grad_out, tn, preferred_element_type=jnp.float32)
        for s in range(slots):
            dk_ref[picks[s], cols] += key_slots[s * TILE : (s + 1) * TILE]
            dv_ref[picks[s], cols] += value_slots[s * TILE : (s + 1) * TILE]
        return carry

    lax.fori_loop(0, heads * tiles, step, 0)


def attend(pool_index, query_rows, grad_rows, pool_keys, pool_values):
    count, width = query_rows.shape
    pool_rows = pool_keys.shape[0]
    slots = pool_index.shape[-1]
    vmem = pltpu.VMEM
    flops = 2 * 7 * count * slots * TILE * width
    return pl.pallas_call(
        attention_kernel,
        out_shape=(
            jax.ShapeDtypeStruct((count, width), jnp.bfloat16),
            jax.ShapeDtypeStruct((count, width), jnp.bfloat16),
            jax.ShapeDtypeStruct((pool_rows, width), jnp.float32),
            jax.ShapeDtypeStruct((pool_rows, width), jnp.float32),
        ),
        in_specs=[pl.BlockSpec(memory_space=pltpu.SMEM)] + [pl.BlockSpec(memory_space=vmem)] * 4,
        out_specs=tuple(pl.BlockSpec(memory_space=vmem) for _ in range(4)),
        scratch_shapes=[
            pltpu.VMEM((slots * TILE, HD), jnp.bfloat16),
            pltpu.VMEM((slots * TILE, HD), jnp.bfloat16),
        ],
        compiler_params=pltpu.CompilerParams(vmem_limit_bytes=60 * 1024 * 1024),
        cost_estimate=pl.CostEstimate(
            flops=flops,
            transcendentals=count * slots * TILE * width // HD,
            bytes_accessed=8 * count * width + 12 * pool_rows * width,
        ),
    )(pool_index.reshape(-1), query_rows, grad_rows, pool_keys, pool_values)


def per_device(query, keys, values, cotangent, kv_tiles):
    head_count = lax.axis_size("head")
    cycle_pos = lax.axis_index("blk")
    per_frame = query.shape[0] * head_count // TILE
    reach = -(-HALF // per_frame)
    span = (2 * reach + 1) * per_frame
    global_tiles = kv_tiles[:, 0, :GLOBALS]
    own_tiles = lax.dynamic_slice_in_dim(kv_tiles, cycle_pos * per_frame, per_frame, 1)
    moved_kv = lax.all_to_all(
        jnp.stack([keys, values]), "head", split_axis=2, concat_axis=1, tiled=True
    )
    moved_qg = lax.all_to_all(
        jnp.stack([query, cotangent]), "head", split_axis=2, concat_axis=1, tiled=True
    )
    moved = (moved_qg[0], moved_kv[0], moved_kv[1], moved_qg[1])
    frame_keys = moved[1]
    frame_values = moved[2]
    offset = 1
    frame_both = jnp.stack([frame_keys, frame_values])
    earlier = passed_along(frame_both, "blk", offset)
    later = passed_along(frame_both, "blk", -offset)
    earlier_keys = [earlier[0]]
    earlier_values = [earlier[1]]
    later_keys = [later[0]]
    later_values = [later[1]]
    near_keys = jnp.stack(earlier_keys[::-1] + later_keys, axis=0)
    near_values = jnp.stack(earlier_values[::-1] + later_values, axis=0)
    width = frame_keys.shape[1]
    all_keys = jnp.concatenate(
        [near_keys[:reach], frame_keys[None], near_keys[reach:]], axis=0
    ).reshape(span * TILE, width)
    all_values = jnp.concatenate(
        [near_values[:reach], frame_values[None], near_values[reach:]], axis=0
    ).reshape(span * TILE, width)
    heads = width // HD
    tile_ids = cycle_pos * per_frame + jnp.arange(per_frame, dtype=jnp.int32)
    owner = global_tiles[:, :, None] == tile_ids[None, None, :]
    owner_mask = owner.astype(jnp.bfloat16)
    frame_key_tiles = frame_keys.reshape(per_frame, TILE, heads, HD)
    frame_value_tiles = frame_values.reshape(per_frame, TILE, heads, HD)
    global_keys = jnp.einsum(
        "hjt,tkhd->jkhd", owner_mask, frame_key_tiles, preferred_element_type=jnp.float32
    )
    global_values = jnp.einsum(
        "hjt,tkhd->jkhd", owner_mask, frame_value_tiles, preferred_element_type=jnp.float32
    )
    global_both = butterfly_sum(
        jnp.stack([global_keys.astype(jnp.bfloat16), global_values.astype(jnp.bfloat16)]), "blk", 0
    )
    global_rows = GLOBALS * TILE
    pool_keys = jnp.concatenate([all_keys, global_both[0].reshape(global_rows, width)], axis=0)
    pool_values = jnp.concatenate([all_values, global_both[1].reshape(global_rows, width)], axis=0)
    relative = own_tiles - (cycle_pos - reach) * per_frame
    inside = (relative >= 0) & (relative < span)
    matches = own_tiles[:, :, :, None] == global_tiles[:, None, None, :]
    slot_numbers = jnp.arange(global_tiles.shape[1], dtype=jnp.int32)
    global_slot = jnp.sum(jnp.where(matches, slot_numbers[None, None, None, :], 0), axis=-1)
    pool_index = jnp.where(inside, relative, span + global_slot)
    attended, query_rows, key_pool, value_pool = attend(
        pool_index, moved[0], moved[3], pool_keys, pool_values
    )
    frame_rows = per_frame * TILE
    centre = reach * frame_rows
    key_grad = key_pool[centre : centre + frame_rows]
    value_grad = value_pool[centre : centre + frame_rows]
    offset = 1
    lower = (reach - offset) * frame_rows
    returned = (
        passed_along(
            key_pool[lower : lower + frame_rows].astype(jnp.bfloat16), "blk", -offset
        ).astype(jnp.float32),
        passed_along(
            value_pool[lower : lower + frame_rows].astype(jnp.bfloat16), "blk", -offset
        ).astype(jnp.float32),
    )
    key_grad = key_grad + returned[0]
    value_grad = value_grad + returned[1]
    upper = (reach + offset) * frame_rows
    returned = (
        passed_along(
            key_pool[upper : upper + frame_rows].astype(jnp.bfloat16), "blk", offset
        ).astype(jnp.float32),
        passed_along(
            value_pool[upper : upper + frame_rows].astype(jnp.bfloat16), "blk", offset
        ).astype(jnp.float32),
    )
    key_grad = key_grad + returned[0]
    value_grad = value_grad + returned[1]
    pool_end = span * TILE
    summed = butterfly_sum(
        jnp.stack([key_pool[pool_end:], value_pool[pool_end:]]).reshape(
            2, GLOBALS, TILE, heads, HD
        ),
        "blk",
        1,
    )
    owner_float = owner.astype(jnp.float32)
    key_grad = key_grad + jnp.einsum(
        "hjt,jkhd->tkhd", owner_float, summed[0], precision=lax.Precision.HIGHEST
    ).reshape(frame_rows, width)
    value_grad = value_grad + jnp.einsum(
        "hjt,jkhd->tkhd", owner_float, summed[1], precision=lax.Precision.HIGHEST
    ).reshape(frame_rows, width)
    key_rows = key_grad.astype(jnp.bfloat16)
    value_rows = value_grad.astype(jnp.bfloat16)
    forward_back = lax.all_to_all(
        jnp.stack([attended, query_rows]), "head", split_axis=1, concat_axis=2, tiled=True
    )
    backward_back = lax.all_to_all(
        jnp.stack([key_rows, value_rows]), "head", split_axis=1, concat_axis=2, tiled=True
    )
    results = (forward_back[0], forward_back[1], backward_back[0], backward_back[1])
    return (results[0], results[1], results[2], results[3])


def solution(mesh):
    placed = (
        P(("blk", "head"), None),
        P(("blk", "head"), None),
        P(("blk", "head"), None),
        P(("blk", "head"), None),
        P("head", None, None),
    )
    return jax.shard_map(
        per_device,
        mesh=mesh,
        in_specs=placed,
        out_specs=(
            P(("blk", "head"), None),
            P(("blk", "head"), None),
            P(("blk", "head"), None),
            P(("blk", "head"), None),
        ),
        check_vma=False,
    )
```
